256 devices in a mesh: section: 32 (over z, y_hi, core), tp: 8 (over x, y_lo).
Axes of the slice: x: 4, y: 4 (y_hi: 2, y_lo: 2; y = y_hi * 2 + y_lo), z: 8, core: 2. Of those that a mesh axis runs over, the one named last changes fastest.
Arguments:
- block_input: bfloat16 [32, 2, 128, 4096], P('section', None, None, 'tp'), may hold values from -6 to 6
- incoming: bfloat16 [32, 2, 128, 4096], P('section', None, None, 'tp'), may hold values from -6 to 6
- in_weight: bfloat16 [32, 4096, 3, 4096], P('section', None, None, 'tp'), may hold values from -0.09375 to 0.09375
- short_taps: float32 [32, 7, 3, 4096], P('section', None, None, 'tp'), may hold values from -2.5 to 2.5
- medium_taps: float32 [32, 128, 256], P('section', None, 'tp'), may hold values from -0.625 to 0.625
- skip_weight: float32 [32, 4096], P('section', 'tp'), may hold values from 0.5 to 1.5
Outputs:
- passed: bfloat16 [32, 2, 128, 4096], P('section', None, None, 'tp')
The draws below stay inside these ranges and needn't reach their ends.
All inputs are finite; a program needn't handle non-finite values.
Results may differ from the reference program's by a relative error of at most 0.0049.
Values may be sent and summed in bfloat16 or wider, within the bound.
A program may use at most 128 MiB of HBM per device.

```python
import jax
import jax.numpy as jnp
from jax import lax

D = 4096
GROUP = 16
SLEN = 7
MLEN = 128
MB = 2
TOK = 128
SECTIONS = 32


def steps_of(own_key, shape, split, smallest, high):
    def one(dim, shards_of):
        steps = jax.random.uniform(jax.random.fold_in(jax.random.fold_in(own_key, 6), dim), (shards_of,), jnp.float32, smallest / len(split), high / len(split))
        return jnp.repeat(jnp.exp(steps), shape[dim] // shards_of).reshape((-1,) + (1,) * (len(shape) - dim - 1))

    level = one(*split[0])
    for cut in split[1:]:
        level = level * one(*cut)
    return level


def centred(stream_key, extent, deviation, limit, cuts=(), held_as=jnp.bfloat16):
    drawn = deviation * jax.random.normal(stream_key, extent, jnp.float32)
    if cuts:
        drawn = drawn * steps_of(stream_key, extent, cuts, -0.22, 0.18)
    return jnp.clip(drawn, -limit, limit).astype(held_as)


def setup_inputs(seed: int = 0) -> dict:
    splits = jax.random.split(jax.random.key(seed), 7)
    return {
        "block_input": centred(splits[0], (SECTIONS, MB, TOK, D), 1.0, 6.0, ((0, 32), (3, 8))),
        "incoming": centred(splits[1], (SECTIONS, MB, TOK, D), 1.0, 6.0, ((0, 32), (3, 8))),
        "in_weight": centred(splits[2], (SECTIONS, D, 3, D), D ** -0.5, 0.09375, ((0, 32), (3, 8))),
        "short_taps": centred(splits[3], (SECTIONS, SLEN, 3, D), 0.4, 2.5, ((0, 32), (3, 8)), jnp.float32),
        "medium_taps": centred(splits[4], (SECTIONS, MLEN, D // GROUP), 0.1, 0.625, ((0, 32), (2, 8)), jnp.float32),
        "skip_weight": jnp.clip(0.5 + 1.0 * jax.random.uniform(splits[5], (SECTIONS, D), jnp.float32) ** steps_of(splits[5], (SECTIONS, D), ((0, 32), (1, 8)), -0.2, 0.2), 0.5, 1.5),
    }


def causal_taps(series, taps):
    length = series.shape[1]
    reach = taps.shape[0]
    padded = jnp.pad(series, ((0, 0), (reach - 1, 0), (0, 0), (0, 0)))
    result = jnp.zeros(series.shape, jnp.float32)
    for offset in range(reach):
        first = reach - 1 - offset
        result = result + taps[offset] * padded[:, first:first + length]
    return result

def anti_taps(series, taps):
    length = series.shape[1]
    reach = taps.shape[0]
    padded = jnp.pad(series, ((0, 0), (0, reach - 1), (0, 0), (0, 0)))
    result = jnp.zeros(series.shape, jnp.float32)
    for offset in range(reach):
        result = result + taps[offset] * padded[:, offset:offset + length]
    return result

def toeplitz_of(medium, length):
    places = jnp.arange(length, dtype=jnp.int32)
    lag_table = places[:, None] - places[None, :]
    lag_values = jnp.arange(medium.shape[0], dtype=jnp.int32)
    lag_match = (lag_table[:, :, None] == lag_values[None, None, :]).astype(jnp.float32)
    return jnp.einsum('tsj,jg->tsg', lag_match, medium, precision=lax.Precision.HIGHEST)

def section_grad(block_input, incoming, in_weight, short_taps, medium_taps, skip_weight):
    micro_count, length, model_width = block_input.shape
    groups = medium_taps.shape[1]
    weights = in_weight.reshape(model_width, 3 * model_width)
    flattened = block_input.reshape(micro_count * length, model_width)
    projected = jnp.dot(flattened, weights, preferred_element_type=jnp.float32)
    projected = projected.reshape(micro_count, length, 3, model_width)
    featured = causal_taps(projected, short_taps)
    query = featured[:, :, 0]
    key_part = featured[:, :, 1]
    value_part = featured[:, :, 2]
    product = key_part * value_part
    toeplitz_mat = toeplitz_of(medium_taps, length)
    grouped = product.reshape(micro_count, length, groups, -1)
    mixed = jnp.einsum('tsg,bsgc->btgc', toeplitz_mat, grouped, precision=lax.Precision.HIGHEST)
    mixed = mixed.reshape(micro_count, length, model_width) + skip_weight * product
    upstream = incoming.astype(jnp.float32)
    query_grad = upstream * mixed
    mixed_grad = upstream * query
    grouped_grad = mixed_grad.reshape(micro_count, length, groups, -1)
    product_grad = jnp.einsum('tsg,btgc->bsgc', toeplitz_mat, grouped_grad, precision=lax.Precision.HIGHEST)
    product_grad = product_grad.reshape(micro_count, length, model_width) + skip_weight * mixed_grad
    stream_grad = jnp.stack([query_grad, product_grad * value_part, product_grad * key_part], axis=2)
    conv_grad = anti_taps(stream_grad, short_taps).astype(jnp.bfloat16)
    conv_flat = conv_grad.reshape(micro_count * length, 3 * model_width)
    input_grad = lax.dot_general(conv_flat, weights, (((1,), (1,)), ((), ())), preferred_element_type=jnp.float32)
    input_grad = input_grad.reshape(micro_count, length, model_width)
    return (upstream + input_grad).astype(jnp.bfloat16)

def reference(block_input, incoming, in_weight, short_taps, medium_taps, skip_weight):

    def one_section(bundle):
        return section_grad(*bundle)
    results = lax.map(one_section, (block_input, incoming, in_weight, short_taps, medium_taps, skip_weight))
    return jnp.roll(results, -1, axis=0)
```

```python
import functools

import jax
import jax.numpy as jnp
from jax import lax
from jax.experimental import pallas as pl
from jax.experimental.pallas import tpu as pltpu
from jax.sharding import PartitionSpec as P

MESH = pl.DeviceIdType.MESH
F32 = jnp.float32
BF16 = jnp.bfloat16
PAD = 8


def split_two(value):
    high = value.astype(BF16)
    low = (value - high.astype(F32)).astype(BF16)
    return high, low


def peer_of(me, offset, sign):
    column = lax.rem(lax.div(me, 2) + 4 + sign * (offset // 2 if isinstance(offset, int) else lax.div(offset, 2)), 4)
    row = lax.rem(me + (offset % 2 if isinstance(offset, int) else lax.rem(offset, 2)), 2)
    return column * 2 + row


def kernel(
    sections, x_hbm, inc_hbm, w_hbm, taps_hbm, medium_hbm, skip_hbm, out_hbm,
    xbuf, inc, w, taps, medium, flipped, skip, proj, turn, grad, fwd_t, bwd_t, own, sendbuf, recvbuf, final,
    local_sem, w_sem, ag_send, ag_recv, rs_send, rs_recv, fin_send, fin_recv,
):
    me = lax.axis_index("tp")
    sec = lax.axis_index("section")
    below = lax.rem(sec + sections - 1, sections)
    above = lax.rem(sec + 1, sections)
    micro, length, width = inc.shape
    blocks = width // 128

    def rows_of(device):
        return pl.ds(pl.multiple_of(device * width, width), width)

    small = [
        pltpu.make_async_copy(x_hbm.at[0], xbuf.at[:, 0], local_sem.at[0]),
        pltpu.make_async_copy(medium_hbm.at[0], medium, local_sem.at[1]),
        pltpu.make_async_copy(taps_hbm, taps, local_sem.at[2]),
        pltpu.make_async_copy(skip_hbm, skip, local_sem.at[3]),
        pltpu.make_async_copy(inc_hbm.at[0], inc, local_sem.at[4]),
    ]
    for copy in small[:2]:
        copy.start()

    def w_copy(offset):
        rows = rows_of(peer_of(me, offset, -1))
        return pltpu.make_async_copy(w_hbm.at[0, :, rows, :], w.at[:, rows, :], w_sem.at[offset])

    for offset in range(8):
        w_copy(offset).start()
    for copy in small[2:]:
        copy.start()

    barrier = pltpu.get_barrier_semaphore()
    for offset in range(1, 8):
        pl.semaphore_signal(barrier, inc=1, device_id={"tp": peer_of(me, offset, 1)}, device_id_type=MESH)
    pl.semaphore_signal(barrier, inc=1, device_id={"section": below}, device_id_type=MESH)
    pl.semaphore_signal(barrier, inc=1, device_id={"section": above}, device_id_type=MESH)
    pl.semaphore_wait(barrier, 9)

    def ag_copy(mb, offset):
        return pltpu.make_async_remote_copy(
            src_ref=x_hbm.at[0, mb],
            dst_ref=xbuf.at[mb, offset],
            send_sem=ag_send.at[mb, offset],
            recv_sem=ag_recv.at[mb, offset],
            device_id={"tp": peer_of(me, offset, 1)},
            device_id_type=MESH,
        )

    for mb in range(micro):
        for offset in (1, 2, 6, 3, 7, 4, 5):
            ag_copy(mb, offset).start()

    small[1].wait()
    place_r = lax.broadcasted_iota(jnp.int32, (128, 128), 0)
    place_c = lax.broadcasted_iota(jnp.int32, (128, 128), 1)
    flip = jnp.where(lax.rem(place_r + place_c, 128) == 0, 1.0, 0.0).astype(F32)
    backward = jnp.dot(medium[...], flip, precision=lax.Precision.HIGHEST, preferred_element_type=F32)
    flipped[...] = backward

    def build(group, carry):
        rows = pl.ds(pl.multiple_of(group * 128, 128), 128)
        ahead = jnp.broadcast_to(medium[pl.ds(group, 1), :], (128, 128))
        ahead = pltpu.roll(ahead, 0, 1, stride=1, stride_axis=0)
        high, low = split_two(jnp.where(place_c >= place_r, ahead, 0.0))
        bwd_t[rows, 0:128] = high
        bwd_t[rows, 128:256] = low
        behind = jnp.broadcast_to(flipped[pl.ds(group, 1), :], (128, 128))
        behind = pltpu.roll(behind, 0, 1, stride=1, stride_axis=0)
        high, low = split_two(jnp.where(place_c <= place_r, behind, 0.0))
        fwd_t[rows, 0:128] = high
        fwd_t[rows, 128:256] = low
        return carry

    lax.fori_loop(0, 32, build, 0)

    for part in range(3 * blocks):
        proj[part, 0:PAD, :] = jnp.zeros((PAD, 128), F32)
        turn[part, length : length + PAD, :] = jnp.zeros((PAD, 128), F32)
    for copy in small[2:]:
        copy.wait()
    small[0].wait()

    def gathered(mb, offset, first):
        rows = rows_of(peer_of(me, offset, -1))
        chunk = xbuf[mb, offset]
        for stream in range(3):
            part = jnp.dot(chunk, w[stream, rows, :], preferred_element_type=F32)
            for block in range(blocks):
                piece = part[:, block * 128 : block * 128 + 128]
                where = (stream * blocks + block, pl.ds(PAD, length), slice(None))
                proj[where] = piece if first else proj[where] + piece

    def medium_conv(table, block, value):
        high, low = split_two(value)
        both = jnp.concatenate([high, low], axis=1)
        both = jnp.concatenate([both, both], axis=0)
        rows = pl.ds(pl.multiple_of(block * 1024, 1024), 1024)
        raw = jnp.dot(table[rows, :], both, preferred_element_type=F32)
        lane_group = lax.div(lax.broadcasted_iota(jnp.int32, (length, 128), 1), 16)
        total = raw[0:length, 0:128] + raw[0:length, 128:256]
        for group in range(1, 8):
            first = group * 128
            piece = raw[first : first + length, 0:128] + raw[first : first + length, 128:256]
            total = jnp.where(lane_group == group, piece, total)
        return total

    def mixer(mb):
        def one_block(block, carry):
            lanes = pl.ds(pl.multiple_of(block * 128, 128), 128)

            def featured(stream):
                total = jnp.zeros((length, 128), F32)
                for lag in range(7):
                    tap = taps[lag * 3 + stream, :, lanes]
                    total = total + tap * proj[stream * blocks + block, pl.ds(PAD - lag, length), :]
                return total

            query, key, value = featured(0), featured(1), featured(2)
            gain = skip[:, lanes]
            product = key * value
            mixed = medium_conv(fwd_t, block, product) + gain * product
            upstream = inc[mb, :, lanes].astype(F32)
            mixed_grad = upstream * query
            product_grad = medium_conv(bwd_t, block, mixed_grad) + gain * mixed_grad
            turn[block, 0:length, :] = upstream * mixed
            turn[blocks + block, 0:length, :] = product_grad * value
            turn[2 * blocks + block, 0:length, :] = product_grad * key
            for stream in range(3):
                total = jnp.zeros((length, 128), F32)
                for lag in range(7):
                    tap = taps[lag * 3 + stream, :, lanes]
                    total = total + tap * turn[stream * blocks + block, pl.ds(lag, length), :]
                grad[stream, :, lanes] = total.astype(BF16)
            return carry

        lax.fori_loop(0, blocks, one_block, 0)

    def share(offset):
        rows = rows_of(peer_of(me, offset, 1))
        total = None
        for stream in range(3):
            part = lax.dot_general(
                grad[stream], w[stream, rows, :], (((1,), (1,)), ((), ())), preferred_element_type=F32
            )
            total = part if total is None else total + part
        return total

    def rs_copy(mb, offset):
        return pltpu.make_async_remote_copy(
            src_ref=sendbuf.at[mb, offset - 1],
            dst_ref=recvbuf.at[mb, offset - 1],
            send_sem=rs_send.at[mb, offset],
            recv_sem=rs_recv.at[mb, offset],
            device_id={"tp": peer_of(me, offset, 1)},
            device_id_type=MESH,
        )

    for mb in range(micro):
        if mb == 0:
            w_copy(0).wait()
        gathered(mb, 0, True)

        def step(offset, carry, mb=mb):
            if mb == 0:
                w_copy(offset).wait()
            ag_copy(mb, offset).wait_recv()
            gathered(mb, offset, False)
            return carry

        lax.fori_loop(1, 8, step, 0)
        mixer(mb)

        def push(offset, carry, mb=mb):
            sendbuf[mb, offset - 1] = share(offset).astype(BF16)
            rs_copy(mb, offset).start()
            return carry

        lax.fori_loop(1, 8, push, 0)
        own[mb] = share(0) + inc[mb].astype(F32)

    def fin_copy(mb):
        return pltpu.make_async_remote_copy(
            src_ref=final.at[mb],
            dst_ref=out_hbm.at[0, mb],
            send_sem=fin_send.at[mb],
            recv_sem=fin_recv.at[mb],
            device_id={"section": below},
            device_id_type=MESH,
        )

    for mb in range(micro):
        def collect(offset, carry, mb=mb):
            rs_copy(mb, offset).wait_recv()
            own[mb] = own[mb] + recvbuf[mb, offset - 1].astype(F32)
            return carry

        lax.fori_loop(1, 8, collect, 0)
        final[mb] = own[mb].astype(BF16)
        fin_copy(mb).start()

    for mb in range(micro):
        def drain(offset, carry, mb=mb):
            ag_copy(mb, offset).wait_send()
            rs_copy(mb, offset).wait_send()
            return carry

        lax.fori_loop(1, 8, drain, 0)
    for mb in range(micro):
        fin_copy(mb).wait()


def local(sections, block_input, incoming, in_weight, short_taps, medium_taps, skip_weight):
    _, micro, length, width = block_input.shape
    model_width = in_weight.shape[1]
    lags = short_taps.shape[1]
    groups = medium_taps.shape[2]
    weights = jnp.transpose(in_weight, (0, 2, 1, 3))
    taps = jnp.transpose(short_taps, (1, 2, 0, 3)).reshape(lags * 3, 1, width)
    medium = jnp.transpose(medium_taps, (0, 2, 1))
    parts = 3 * (width // 128)
    anywhere = pl.BlockSpec(memory_space=pl.ANY)
    dma = pltpu.SemaphoreType.DMA
    return pl.pallas_call(
        functools.partial(kernel, sections),
        out_shape=jax.ShapeDtypeStruct(block_input.shape, BF16),
        in_specs=[anywhere] * 6,
        out_specs=anywhere,
        scratch_shapes=[
            pltpu.VMEM((micro, 8, length, width), BF16),
            pltpu.VMEM((micro, length, width), BF16),
            pltpu.VMEM((3, model_width, width), BF16),
            pltpu.VMEM((lags * 3, 1, width), F32),
            pltpu.VMEM((groups, 128), F32),
            pltpu.VMEM((groups, 128), F32),
            pltpu.VMEM((1, width), F32),
            pltpu.VMEM((parts, length + PAD, 128), F32),
            pltpu.VMEM((parts, length + PAD, 128), F32),
            pltpu.VMEM((3, length, width), BF16),
            pltpu.VMEM((groups * 128, 256), BF16),
            pltpu.VMEM((groups * 128, 256), BF16),
            pltpu.VMEM((micro, length, width), F32),
            pltpu.VMEM((micro, 7, length, width), BF16),
            pltpu.VMEM((micro, 7, length, width), BF16),
            pltpu.VMEM((micro, length, width), BF16),
            dma((5,)),
            dma((8,)),
            dma((micro, 8)),
            dma((micro, 8)),
            dma((micro, 8)),
            dma((micro, 8)),
            dma((micro,)),
            dma((micro,)),
        ],
        compiler_params=pltpu.CompilerParams(
            collective_id=0, has_side_effects=True, vmem_limit_bytes=56 * 1024 * 1024
        ),
    )(block_input, incoming, weights, taps, medium, skip_weight)


def solution(mesh):
    in_specs = (
        P("section", None, None, "tp"),
        P("section", None, None, "tp"),
        P("section", None, None, "tp"),
        P("section", None, None, "tp"),
        P("section", None, "tp"),
        P("section", "tp"),
    )
    out_specs = P("section", None, None, "tp")
    return jax.shard_map(
        functools.partial(local, mesh.shape["section"]),
        mesh=mesh, in_specs=in_specs, out_specs=out_specs, check_vma=False,
    )
```

```python
import functools

import jax
import jax.numpy as jnp
from jax import lax
from jax.experimental import pallas as pl
from jax.experimental.pallas import tpu as pltpu
from jax.sharding import PartitionSpec as P

MESH = pl.DeviceIdType.MESH
F32 = jnp.float32
BF16 = jnp.bfloat16
PAD = 8
HALF = 256
RIGHT, LEFT, ACROSS = (1, 0), (3, 0), (0, 1)

ORIGIN = {
    0: [(RIGHT, (1, 0)), (LEFT, (3, 0)), (ACROSS, (0, 1))],
    1: [(ACROSS, (0, 1)), (RIGHT, (1, 0)), (LEFT, (3, 0))],
}


def forwards(mb, cls, key):
    if cls == 0:
        far = RIGHT if mb == 0 else LEFT
        table = {
            (1, 0): [(ACROSS, (1, 1))],
            (3, 0): [(ACROSS, (3, 1))],
            (2, 0): [(ACROSS, (2, 1))],
        }
        table[far].insert(0, (far, (2, 0)))
    else:
        table = {
            (0, 1): [(RIGHT, (1, 1)), (LEFT, (3, 1))],
            (1, 0): [(RIGHT, (2, 0))],
            (3, 1): [(LEFT, (2, 1))],
        }
    return table.get(key, [])


def returns(mb, cls, key):
    if cls == 0:
        far = RIGHT if mb == 0 else LEFT
        if key[1] == 1:
            return ACROSS, []
        if key == (2, 0):
            return far, [(2, 1)]
        if key == (0, 0):
            return None, [(0, 1), (1, 0), (3, 0)]
        return key, [(key[0], 1)] + ([(2, 0)] if key == far else [])
    return {
        (2, 0): (RIGHT, []),
        (2, 1): (LEFT, []),
        (1, 1): (RIGHT, []),
        (3, 0): (LEFT, []),
        (1, 0): (RIGHT, [(2, 0)]),
        (3, 1): (LEFT, [(2, 1)]),
        (0, 1): (ACROSS, [(1, 1), (3, 1)]),
        (0, 0): (None, [(3, 0), (1, 0), (0, 1)]),
    }[key]


def slot(key):
    return key[0] * 2 + key[1]


def split_two(value):
    high = value.astype(BF16)
    low = (value - high.astype(F32)).astype(BF16)
    return high, low


def kernel(
    sections, x_hbm, inc_hbm, w_hbm, taps_hbm, medium_hbm, skip_hbm, out_hbm,
    xbuf, inc, w, taps, medium, flipped, skip, proj, turn, grad_t, fwd_t, bwd_t, partial, sendbuf, recvbuf, final,
    local_sem, w_sem, ag_send, ag_recv, rs_send, rs_recv, fin_send, fin_recv,
):
    me = lax.axis_index("tp")
    sec = lax.axis_index("section")
    below = lax.rem(sec + sections - 1, sections)
    above = lax.rem(sec + 1, sections)
    micro, length, width = inc.shape
    blocks = width // 128
    column, row = lax.div(me, 2), lax.rem(me, 2)

    def device_at(dx, dy):
        return lax.rem(column + 4 + dx, 4) * 2 + lax.rem(row + dy, 2)

    def rows_of(device, start, size):
        return pl.ds(pl.multiple_of(device * width + start, HALF), size)

    small = [
        pltpu.make_async_copy(medium_hbm.at[0], medium, local_sem.at[0]),
        pltpu.make_async_copy(taps_hbm, taps, local_sem.at[1]),
        pltpu.make_async_copy(skip_hbm, skip, local_sem.at[2]),
        pltpu.make_async_copy(inc_hbm.at[0], inc, local_sem.at[3]),
    ]
    own_x = [
        [
            pltpu.make_async_copy(
                x_hbm.at[0, mb, :, pl.ds(cls * HALF, HALF)], xbuf.at[mb, cls, 0], local_sem.at[4 + mb * 2 + cls]
            )
            for cls in range(2)
        ]
        for mb in range(micro)
    ]

    def w_copy(key):
        rows = rows_of(device_at(-key[0], key[1]), 0, width)
        return pltpu.make_async_copy(w_hbm.at[0, :, rows, :], w.at[:, rows, :], w_sem.at[slot(key)])

    barrier = pltpu.get_barrier_semaphore()
    for hop in (RIGHT, LEFT, ACROSS):
        pl.semaphore_signal(barrier, inc=1, device_id={"tp": device_at(*hop)}, device_id_type=MESH)
    pl.semaphore_signal(barrier, inc=1, device_id={"section": below}, device_id_type=MESH)
    pl.semaphore_signal(barrier, inc=1, device_id={"section": above}, device_id_type=MESH)
    for mb in range(micro):
        for cls in range(2):
            own_x[mb][cls].start()
    small[0].start()
    arrival = [(0, 0), (0, 1), (1, 0), (3, 0), (3, 1), (2, 0), (1, 1), (2, 1)]
    for key in arrival:
        w_copy(key).start()
    for copy in small[1:]:
        copy.start()

    place_r = lax.broadcasted_iota(jnp.int32, (128, 128), 0)
    place_c = lax.broadcasted_iota(jnp.int32, (128, 128), 1)
    small[0].wait()
    flip = jnp.where(lax.rem(place_r + place_c, 128) == 0, 1.0, 0.0).astype(F32)
    flipped[...] = jnp.dot(medium[...], flip, precision=lax.Precision.HIGHEST, preferred_element_type=F32)
    for part in range(3 * blocks):
        proj[part, 0:PAD, :] = jnp.zeros((PAD, 128), F32)
        turn[part, length : length + PAD, :] = jnp.zeros((PAD, 128), F32)
    for mb in range(micro):
        for cls in range(2):
            own_x[mb][cls].wait()

    pl.semaphore_wait(barrier, 5)

    sent = []

    def gather_copy(mb, cls, source, hop, key):
        return pltpu.make_async_remote_copy(
            src_ref=xbuf.at[mb, cls, slot(source)],
            dst_ref=xbuf.at[mb, cls, slot(key)],
            send_sem=ag_send.at[mb, cls, slot(key)],
            recv_sem=ag_recv.at[mb, cls, slot(key)],
            device_id={"tp": device_at(*hop)},
            device_id_type=MESH,
        )

    def gather_start(mb):
        for cls in (1, 0):
            for hop, key in ORIGIN[cls]:
                copy = gather_copy(mb, cls, (0, 0), hop, key)
                copy.start()
                sent.append(copy)

    def gather_handle(mb, *units):
        for cls, key in units:
            gather_copy(mb, cls, (0, 0), RIGHT, key).wait_recv()
            for hop, there in forwards(mb, cls, key):
                copy = gather_copy(mb, cls, key, hop, there)
                copy.start()
                sent.append(copy)

    def project(mb, units, first=False):
        for stream in range(3):
            total = None
            for cls, key in units:
                rows = rows_of(device_at(-key[0], key[1]), cls * HALF, HALF)
                part = jnp.dot(xbuf[mb, cls, slot(key)], w[stream, rows, :], preferred_element_type=F32)
                total = part if total is None else total + part
            for block in range(blocks):
                piece = total[:, block * 128 : block * 128 + 128]
                where = (stream * blocks + block, pl.ds(PAD, length), slice(None))
                proj[where] = piece if first else proj[where] + piece

    def build_tables(begin, end):
        def build(group, carry):
            rows = pl.ds(pl.multiple_of(group * 128, 128), 128)
            ahead = jnp.broadcast_to(medium[pl.ds(group, 1), :], (128, 128))
            ahead = pltpu.roll(ahead, 0, 1, stride=1, stride_axis=0)
            high, low = split_two(jnp.where(place_c >= place_r, ahead, 0.0))
            bwd_t[rows, 0:128] = high
            bwd_t[rows, 128:256] = low
            behind = jnp.broadcast_to(flipped[pl.ds(group, 1), :], (128, 128))
            behind = pltpu.roll(behind, 0, 1, stride=1, stride_axis=0)
            high, low = split_two(jnp.where(place_c <= place_r, behind, 0.0))
            fwd_t[rows, 0:128] = high
            fwd_t[rows, 128:256] = low
            return carry

        lax.fori_loop(begin, end, build, 0)

    def medium_conv(table, block, value):
        high, low = split_two(value)
        both = jnp.concatenate([high, low], axis=1)
        both = jnp.concatenate([both, both], axis=0)
        rows = pl.ds(pl.multiple_of(block * 1024, 1024), 1024)
        raw = jnp.dot(table[rows, :], both, preferred_element_type=F32)
        lane_group = lax.div(place_c, 16)
        total = raw[0:length, 0:128] + raw[0:length, 128:256]
        for group in range(1, 8):
            first = group * 128
            piece = raw[first : first + length, 0:128] + raw[first : first + length, 128:256]
            total = jnp.where(lane_group == group, piece, total)
        return total

    def mixer(mb, begin, end):
        def one_block(block, carry):
            lanes = pl.ds(pl.multiple_of(block * 128, 128), 128)

            def featured(stream):
                total = jnp.zeros((length, 128), F32)
                for lag in range(7):
                    tap = taps[lag * 3 + stream, :, lanes]
                    total = total + tap * proj[stream * blocks + block, pl.ds(PAD - lag, length), :]
                return total

            query, key, value = featured(0), featured(1), featured(2)
            gain = skip[:, lanes]
            product = key * value
            mixed = medium_conv(fwd_t, block, product) + gain * product
            upstream = inc[mb, :, lanes].astype(F32)
            mixed_grad = upstream * query
            product_grad = medium_conv(bwd_t, block, mixed_grad) + gain * mixed_grad
            turn[block, 0:length, :] = upstream * mixed
            turn[blocks + block, 0:length, :] = product_grad * value
            turn[2 * blocks + block, 0:length, :] = product_grad * key
            for stream in range(3):
                total = jnp.zeros((length, 128), F32)
                for lag in range(7):
                    tap = taps[lag * 3 + stream, :, lanes]
                    total = total + tap * turn[stream * blocks + block, pl.ds(lag, length), :]
                rows = pl.ds(pl.multiple_of(stream * width + block * 128, 128), 128)
                grad_t[rows, :] = jnp.transpose(total).astype(BF16)
            return carry

        lax.fori_loop(begin, end, one_block, 0)

    def sum_copy(mb, cls, key, hop):
        return pltpu.make_async_remote_copy(
            src_ref=sendbuf.at[mb, cls, slot(key)],
            dst_ref=recvbuf.at[mb, cls, slot(key)],
            send_sem=rs_send.at[mb, cls, slot(key)],
            recv_sem=rs_recv.at[mb, cls, slot(key)],
            device_id={"tp": device_at(*hop)},
            device_id_type=MESH,
        )

    def push_sum(mb, cls, key, hop, value):
        sendbuf[mb, cls, slot(key)] = value.astype(BF16)
        copy = sum_copy(mb, cls, key, hop)
        copy.start()
        sent.append(copy)

    def share(mb, *keys):
        for key in keys:
            rows = rows_of(device_at(*key), 0, width)
            total = None
            for stream in range(3):
                part = jnp.dot(
                    w[stream, rows, :], grad_t[stream * width : stream * width + width, :], preferred_element_type=F32
                )
                total = part if total is None else total + part
            for cls in range(2):
                piece = total[cls * HALF : cls * HALF + HALF, :]
                hop, joins = returns(mb, cls, key)
                if hop is not None and not joins:
                    push_sum(mb, cls, key, hop, piece)
                else:
                    partial[cls, slot(key)] = piece

    def combine(mb, cls, key):
        hop, joins = returns(mb, cls, key)
        total = partial[cls, slot(key)]
        for join in joins:
            sum_copy(mb, cls, join, RIGHT).wait_recv()
            total = total + recvbuf[mb, cls, slot(join)].astype(F32)
        if hop is not None:
            push_sum(mb, cls, key, hop, total)
            return
        upstream = inc[mb, :, cls * HALF : cls * HALF + HALF].astype(F32)
        final[mb, cls] = (jnp.transpose(total) + upstream).astype(BF16)
        copy = pltpu.make_async_remote_copy(
            src_ref=final.at[mb, cls],
            dst_ref=out_hbm.at[0, mb, :, pl.ds(cls * HALF, HALF)],
            send_sem=fin_send.at[mb, cls],
            recv_sem=fin_recv.at[mb, cls],
            device_id={"section": below},
            device_id_type=MESH,
        )
        copy.start()
        ended.append(copy)

    ended = []
    group_a = [(1, (0, 1)), (0, (1, 0)), (0, (3, 0)), (1, (1, 0))]
    group_b = [(1, (3, 1)), (0, (2, 0))]
    group_c = [(1, (3, 0)), (0, (0, 1))]
    group_d = [(1, (1, 1)), (0, (1, 1)), (0, (3, 1)), (1, (2, 0))]
    group_e = [(1, (2, 1)), (0, (2, 1))]
    owned = [(0, (0, 0)), (1, (0, 0))]

    gather_start(0)
    build_tables(0, 12)
    w_copy((0, 0)).wait()
    project(0, owned, first=True)
    gather_handle(0, *group_a)
    gather_start(1)
    for key in arrival[1:]:
        w_copy(key).wait()
    project(0, group_a)
    gather_handle(0, *group_b)
    build_tables(12, 22)
    gather_handle(0, *group_c)
    project(0, group_b + group_c)
    build_tables(22, 32)
    gather_handle(0, *group_d)
    project(0, group_d)
    gather_handle(1, *group_a)
    gather_handle(0, *group_e)
    project(0, group_e)
    for copy in small[1:]:
        copy.wait()
    mixer(0, 0, 2)
    gather_handle(1, *group_b)
    mixer(0, 2, 4)
    share(0, (2, 1), (2, 0), (1, 1), (3, 1), (0, 1), (3, 0), (1, 0), (0, 0))
    project(1, owned, first=True)
    project(1, group_a)
    combine(0, 0, (2, 0))
    combine(0, 1, (1, 0))
    combine(0, 1, (3, 1))
    gather_handle(1, *group_c)
    project(1, group_b + group_c)
    combine(0, 0, (3, 0))
    combine(0, 0, (1, 0))
    combine(0, 1, (0, 1))
    gather_handle(1, *group_d)
    project(1, group_d)
    gather_handle(1, *group_e)
    project(1, group_e)
    mixer(1, 0, 2)
    combine(0, 0, (0, 0))
    combine(0, 1, (0, 0))
    mixer(1, 2, 4)
    share(1, (2, 1), (2, 0), (1, 1), (3, 1))
    combine(1, 0, (2, 0))
    combine(1, 1, (3, 1))
    share(1, (0, 1), (3, 0), (1, 0))
    combine(1, 1, (1, 0))
    combine(1, 0, (1, 0))
    combine(1, 0, (3, 0))
    combine(1, 1, (0, 1))
    share(1, (0, 0))
    combine(1, 0, (0, 0))
    combine(1, 1, (0, 0))
    for copy in sent:
        copy.wait_send()
    for copy in ended:
        copy.wait()


def local(sections, block_input, incoming, in_weight, short_taps, medium_taps, skip_weight):
    _, micro, length, width = block_input.shape
    model_width = in_weight.shape[1]
    lags = short_taps.shape[1]
    groups = medium_taps.shape[2]
    weights = jnp.transpose(in_weight, (0, 2, 1, 3))
    taps = jnp.transpose(short_taps, (1, 2, 0, 3)).reshape(lags * 3, 1, width)
    medium = jnp.transpose(medium_taps, (0, 2, 1))
    parts = 3 * (width // 128)
    anywhere = pl.BlockSpec(memory_space=pl.ANY)
    dma = pltpu.SemaphoreType.DMA
    return pl.pallas_call(
        functools.partial(kernel, sections),
        out_shape=jax.ShapeDtypeStruct(block_input.shape, BF16),
        in_specs=[anywhere] * 6,
        out_specs=anywhere,
        scratch_shapes=[
            pltpu.VMEM((micro, 2, 8, length, HALF), BF16),
            pltpu.VMEM((micro, length, width), BF16),
            pltpu.VMEM((3, model_width, width), BF16),
            pltpu.VMEM((lags * 3, 1, width), F32),
            pltpu.VMEM((groups, 128), F32),
            pltpu.VMEM((groups, 128), F32),
            pltpu.VMEM((1, width), F32),
            pltpu.VMEM((parts, length + PAD, 128), F32),
            pltpu.VMEM((parts, length + PAD, 128), F32),
            pltpu.VMEM((3 * width, length), BF16),
            pltpu.VMEM((groups * 128, 256), BF16),
            pltpu.VMEM((groups * 128, 256), BF16),
            pltpu.VMEM((2, 8, HALF, length), F32),
            pltpu.VMEM((micro, 2, 8, HALF, length), BF16),
            pltpu.VMEM((micro, 2, 8, HALF, length), BF16),
            pltpu.VMEM((micro, 2, length, HALF), BF16),
            dma((8,)),
            dma((8,)),
            dma((micro, 2, 8)),
            dma((micro, 2, 8)),
            dma((micro, 2, 8)),
            dma((micro, 2, 8)),
            dma((micro, 2)),
            dma((micro, 2)),
        ],
        compiler_params=pltpu.CompilerParams(
            collective_id=0, has_side_effects=True, vmem_limit_bytes=56 * 1024 * 1024
        ),
    )(block_input, incoming, weights, taps, medium, skip_weight)


def solution(mesh):
    in_specs = (
        P("section", None, None, "tp"),
        P("section", None, None, "tp"),
        P("section", None, None, "tp"),
        P("section", None, None, "tp"),
        P("section", None, "tp"),
        P("section", "tp"),
    )
    out_specs = P("section", None, None, "tp")
    return jax.shard_map(
        functools.partial(local, mesh.shape["section"]),
        mesh=mesh, in_specs=in_specs, out_specs=out_specs, check_vma=False,
    )
```

```python
import functools

import jax
import jax.numpy as jnp
from jax import lax
from jax.experimental import pallas as pl
from jax.experimental.pallas import tpu as pltpu
from jax.sharding import PartitionSpec as P

MESH = pl.DeviceIdType.MESH
F32 = jnp.float32
BF16 = jnp.bfloat16
PAD = 8
HALF = 256
RIGHT, LEFT, ACROSS = (1, 0), (3, 0), (0, 1)

ORIGIN = {
    0: [(RIGHT, (1, 0)), (LEFT, (3, 0)), (ACROSS, (0, 1))],
    1: [(ACROSS, (0, 1)), (RIGHT, (1, 0)), (LEFT, (3, 0))],
}


def forwards(mb, cls, key):
    if cls == 0:
        far = RIGHT if mb == 0 else LEFT
        table = {
            (1, 0): [(ACROSS, (1, 1))],
            (3, 0): [(ACROSS, (3, 1))],
            (2, 0): [(ACROSS, (2, 1))],
        }
        table[far].insert(0, (far, (2, 0)))
    else:
        table = {
            (0, 1): [(RIGHT, (1, 1)), (LEFT, (3, 1))],
            (1, 0): [(RIGHT, (2, 0))],
            (3, 1): [(LEFT, (2, 1))],
        }
    return table.get(key, [])


def returns(mb, cls, key):
    if cls == 0:
        far = RIGHT if mb == 0 else LEFT
        if key[1] == 1:
            return ACROSS, []
        if key == (2, 0):
            return far, [(2, 1)]
        if key == (0, 0):
            return None, [(0, 1), (1, 0), (3, 0)]
        return key, [(key[0], 1)] + ([(2, 0)] if key == far else [])
    return {
        (2, 0): (RIGHT, []),
        (2, 1): (LEFT, []),
        (1, 1): (RIGHT, []),
        (3, 0): (LEFT, []),
        (1, 0): (RIGHT, [(2, 0)]),
        (3, 1): (LEFT, [(2, 1)]),
        (0, 1): (ACROSS, [(1, 1), (3, 1)]),
        (0, 0): (None, [(3, 0), (1, 0), (0, 1)]),
    }[key]


def slot(key):
    return key[0] * 2 + key[1]


def split_two(value):
    high = value.astype(BF16)
    low = (value - high.astype(F32)).astype(BF16)
    return high, low


def kernel(
    sections, x_hbm, inc_hbm, w_hbm, taps_hbm, medium_hbm, skip_hbm, out_hbm,
    xbuf, inc, w, taps, medium, flipped, skip, proj, turn, grad_t, fwd_t, bwd_t, partial, sendbuf, recvbuf, final,
    local_sem, w_sem, ag_send, ag_recv, rs_send, rs_recv, fin_send, fin_recv,
):
    me = lax.axis_index("tp")
    sec = lax.axis_index("section")
    below = lax.rem(sec + sections - 1, sections)
    above = lax.rem(sec + 1, sections)
    micro, length, width = inc.shape
    blocks = width // 128
    column, row = lax.div(me, 2), lax.rem(me, 2)

    def device_at(dx, dy):
        return lax.rem(column + 4 + dx, 4) * 2 + lax.rem(row + dy, 2)

    def rows_of(device, start, size):
        return pl.ds(pl.multiple_of(device * width + start, HALF), size)

    small = [
        pltpu.make_async_copy(medium_hbm.at[0], medium, local_sem.at[0]),
        pltpu.make_async_copy(taps_hbm, taps, local_sem.at[1]),
        pltpu.make_async_copy(skip_hbm, skip, local_sem.at[2]),
        pltpu.make_async_copy(inc_hbm.at[0], inc, local_sem.at[3]),
    ]
    own_x = [
        [
            pltpu.make_async_copy(
                x_hbm.at[0, mb, :, pl.ds(cls * HALF, HALF)], xbuf.at[mb, cls, 0], local_sem.at[4 + mb * 2 + cls]
            )
            for cls in range(2)
        ]
        for mb in range(micro)
    ]

    def w_copy(key):
        rows = rows_of(device_at(-key[0], key[1]), 0, width)
        return pltpu.make_async_copy(w_hbm.at[0, :, rows, :], w.at[:, rows, :], w_sem.at[slot(key)])

    barrier = pltpu.get_barrier_semaphore()
    for hop in (RIGHT, LEFT, ACROSS):
        pl.semaphore_signal(barrier, inc=1, device_id={"tp": device_at(*hop)}, device_id_type=MESH)
    pl.semaphore_signal(barrier, inc=1, device_id={"section": below}, device_id_type=MESH)
    pl.semaphore_signal(barrier, inc=1, device_id={"section": above}, device_id_type=MESH)
    for mb in range(micro):
        for cls in range(2):
            own_x[mb][cls].start()
    small[0].start()
    arrival = [(0, 0), (0, 1), (1, 0), (3, 0), (1, 1), (3, 1), (2, 0), (2, 1)]
    for key in arrival:
        w_copy(key).start()
    for copy in small[1:]:
        copy.start()

    place_r = lax.broadcasted_iota(jnp.int32, (128, 128), 0)
    place_c = lax.broadcasted_iota(jnp.int32, (128, 128), 1)
    small[0].wait()
    flip = jnp.where(lax.rem(place_r + place_c, 128) == 0, 1.0, 0.0).astype(F32)
    flipped[...] = jnp.dot(medium[...], flip, precision=lax.Precision.HIGHEST, preferred_element_type=F32)
    for part in range(3 * blocks):
        for mb in range(micro):
            proj[mb, part, 0:PAD, :] = jnp.zeros((PAD, 128), F32)
        turn[part, length : length + PAD, :] = jnp.zeros((PAD, 128), F32)
    for mb in range(micro):
        for cls in range(2):
            own_x[mb][cls].wait()

    pl.semaphore_wait(barrier, 5)

    sent = []

    def gather_copy(mb, cls, source, hop, key):
        return pltpu.make_async_remote_copy(
            src_ref=xbuf.at[mb, cls, slot(source)],
            dst_ref=xbuf.at[mb, cls, slot(key)],
            send_sem=ag_send.at[mb, cls, slot(key)],
            recv_sem=ag_recv.at[mb, cls, slot(key)],
            device_id={"tp": device_at(*hop)},
            device_id_type=MESH,
        )

    def origin(mb, cls, number):
        hop, key = ORIGIN[cls][number]
        copy = gather_copy(mb, cls, (0, 0), hop, key)
        copy.start()
        sent.append(copy)

    def handle(mb, cls, dx, dy):
        gather_copy(mb, cls, (0, 0), RIGHT, (dx, dy)).wait_recv()
        for hop, there in forwards(mb, cls, (dx, dy)):
            copy = gather_copy(mb, cls, (dx, dy), hop, there)
            copy.start()
            sent.append(copy)

    loaded, begun = set(), set()

    def project(mb, dx, dy):
        if (dx, dy) not in loaded:
            w_copy((dx, dy)).wait()
            loaded.add((dx, dy))
        rows = rows_of(device_at(-dx, dy), 0, width)
        chunk = jnp.concatenate([xbuf[mb, 0, slot((dx, dy))], xbuf[mb, 1, slot((dx, dy))]], axis=1)
        for stream in range(3):
            total = jnp.dot(chunk, w[stream, rows, :], preferred_element_type=F32)
            for block in range(blocks):
                piece = total[:, block * 128 : block * 128 + 128]
                where = (mb, stream * blocks + block, pl.ds(PAD, length), slice(None))
                proj[where] = proj[where] + piece if mb in begun else piece
        begun.add(mb)

    def build_tables(number):
        def build(group, carry):
            rows = pl.ds(pl.multiple_of(group * 128, 128), 128)
            ahead = jnp.broadcast_to(medium[pl.ds(group, 1), :], (128, 128))
            ahead = pltpu.roll(ahead, 0, 1, stride=1, stride_axis=0)
            high, low = split_two(jnp.where(place_c >= place_r, ahead, 0.0))
            bwd_t[rows, 0:128] = high
            bwd_t[rows, 128:256] = low
            behind = jnp.broadcast_to(flipped[pl.ds(group, 1), :], (128, 128))
            behind = pltpu.roll(behind, 0, 1, stride=1, stride_axis=0)
            high, low = split_two(jnp.where(place_c <= place_r, behind, 0.0))
            fwd_t[rows, 0:128] = high
            fwd_t[rows, 128:256] = low
            return carry

        lax.fori_loop(4 * number, 4 * number + 4, build, 0)

    def medium_conv(table, block, value):
        high, low = split_two(value)
        both = jnp.concatenate([high, low], axis=1)
        both = jnp.concatenate([both, both], axis=0)
        rows = pl.ds(pl.multiple_of(block * 1024, 1024), 1024)
        raw = jnp.dot(table[rows, :], both, preferred_element_type=F32)
        lane_group = lax.div(place_c, 16)
        total = raw[0:length, 0:128] + raw[0:length, 128:256]
        for group in range(1, 8):
            first = group * 128
            piece = raw[first : first + length, 0:128] + raw[first : first + length, 128:256]
            total = jnp.where(lane_group == group, piece, total)
        return total

    ready = []

    def mixer(mb, half):
        while len(ready) < len(small) - 1:
            ready.append(small[len(ready) + 1].wait())

        def one_block(block, carry):
            lanes = pl.ds(pl.multiple_of(block * 128, 128), 128)

            def featured(stream):
                total = jnp.zeros((length, 128), F32)
                for lag in range(7):
                    tap = taps[lag * 3 + stream, :, lanes]
                    total = total + tap * proj[mb, stream * blocks + block, pl.ds(PAD - lag, length), :]
                return total

            query, key, value = featured(0), featured(1), featured(2)
            gain = skip[:, lanes]
            product = key * value
            mixed = medium_conv(fwd_t, block, product) + gain * product
            upstream = inc[mb, :, lanes].astype(F32)
            mixed_grad = upstream * query
            product_grad = medium_conv(bwd_t, block, mixed_grad) + gain * mixed_grad
            turn[block, 0:length, :] = upstream * mixed
            turn[blocks + block, 0:length, :] = product_grad * value
            turn[2 * blocks + block, 0:length, :] = product_grad * key
            for stream in range(3):
                total = jnp.zeros((length, 128), F32)
                for lag in range(7):
                    tap = taps[lag * 3 + stream, :, lanes]
                    total = total + tap * turn[stream * blocks + block, pl.ds(lag, length), :]
                rows = pl.ds(pl.multiple_of(stream * width + block * 128, 128), 128)
                grad_t[mb, rows, :] = jnp.transpose(total).astype(BF16)
            return carry

        lax.fori_loop(2 * half, 2 * half + 2, one_block, 0)

    def sum_copy(mb, cls, key, hop):
        return pltpu.make_async_remote_copy(
            src_ref=sendbuf.at[mb, cls, slot(key)],
            dst_ref=recvbuf.at[mb, cls, slot(key)],
            send_sem=rs_send.at[mb, cls, slot(key)],
            recv_sem=rs_recv.at[mb, cls, slot(key)],
            device_id={"tp": device_at(*hop)},
            device_id_type=MESH,
        )

    def push_sum(mb, cls, key, hop, value):
        sendbuf[mb, cls, slot(key)] = value.astype(BF16)
        copy = sum_copy(mb, cls, key, hop)
        copy.start()
        sent.append(copy)

    def share(mb, dx, dy):
        key = (dx, dy)
        rows = rows_of(device_at(*key), 0, width)
        total = None
        for stream in range(3):
            part = jnp.dot(
                w[stream, rows, :], grad_t[mb, stream * width : stream * width + width, :], preferred_element_type=F32
            )
            total = part if total is None else total + part
        for cls in range(2):
            piece = total[cls * HALF : cls * HALF + HALF, :]
            hop, joins = returns(mb, cls, key)
            if hop is not None and not joins:
                push_sum(mb, cls, key, hop, piece)
            else:
                partial[mb, cls, slot(key)] = piece

    def combine(mb, cls, dx, dy):
        key = (dx, dy)
        hop, joins = returns(mb, cls, key)
        total = partial[mb, cls, slot(key)]
        for join in joins:
            sum_copy(mb, cls, join, RIGHT).wait_recv()
            total = total + recvbuf[mb, cls, slot(join)].astype(F32)
        if hop is not None:
            push_sum(mb, cls, key, hop, total)
            return
        upstream = inc[mb, :, cls * HALF : cls * HALF + HALF].astype(F32)
        final[mb, cls] = (jnp.transpose(total) + upstream).astype(BF16)
        copy = pltpu.make_async_remote_copy(
            src_ref=final.at[mb, cls],
            dst_ref=out_hbm.at[0, mb, :, pl.ds(cls * HALF, HALF)],
            send_sem=fin_send.at[mb, cls],
            recv_sem=fin_recv.at[mb, cls],
            device_id={"section": below},
            device_id_type=MESH,
        )
        copy.start()
        ended.append(copy)

    ended = []
    origin(1, 0, 1)
    origin(1, 1, 0)
    origin(1, 0, 0)
    origin(0, 0, 0)
    origin(1, 1, 2)
    origin(1, 1, 1)
    origin(0, 0, 1)
    build_tables(1)
    origin(0, 0, 2)
    build_tables(0)
    origin(0, 1, 0)
    build_tables(3)
    origin(1, 0, 2)
    handle(1, 0, 3, 0)
    handle(1, 1, 0, 1)
    build_tables(2)
    origin(0, 1, 2)
    handle(1, 0, 1, 0)
    build_tables(4)
    project(1, 0, 0)
    origin(0, 1, 1)
    handle(0, 0, 0, 1)
    project(0, 0, 0)
    handle(0, 0, 1, 0)
    handle(1, 1, 1, 0)
    build_tables(6)
    handle(0, 1, 0, 1)
    handle(1, 0, 2, 0)
    project(0, 0, 1)
    build_tables(5)
    handle(0, 0, 3, 0)
    handle(1, 1, 3, 1)
    handle(0, 1, 1, 0)
    handle(1, 0, 3, 1)
    project(1, 1, 0)
    handle(1, 1, 3, 0)
    project(0, 1, 0)
    handle(0, 1, 3, 0)
    handle(1, 0, 0, 1)
    project(1, 3, 1)
    handle(1, 0, 1, 1)
    project(0, 3, 0)
    project(1, 0, 1)
    build_tables(7)
    handle(0, 0, 2, 0)
    handle(0, 1, 3, 1)
    handle(1, 1, 1, 1)
    project(1, 3, 0)
    handle(1, 1, 2, 0)
    project(1, 1, 1)
    project(1, 2, 0)
    handle(1, 0, 2, 1)
    handle(1, 1, 2, 1)
    project(1, 2, 1)
    mixer(1, 1)
    handle(0, 0, 3, 1)
    handle(0, 1, 1, 1)
    mixer(1, 0)
    handle(0, 0, 1, 1)
    handle(0, 1, 2, 0)
    project(0, 1, 1)
    handle(0, 0, 2, 1)
    project(0, 3, 1)
    share(1, 2, 1)
    project(0, 2, 0)
    handle(0, 1, 2, 1)
    share(1, 1, 1)
    project(0, 2, 1)
    mixer(0, 0)
    mixer(0, 1)
    share(0, 2, 1)
    share(1, 2, 0)
    combine(1, 0, 2, 0)
    share(1, 3, 1)
    share(0, 1, 1)
    share(1, 1, 0)
    share(0, 2, 0)
    combine(1, 1, 3, 1)
    share(0, 3, 1)
    combine(1, 0, 1, 0)
    share(1, 0, 1)
    combine(0, 1, 3, 1)
    share(1, 3, 0)
    combine(0, 0, 2, 0)
    share(0, 0, 1)
    combine(1, 1, 1, 0)
    combine(1, 0, 3, 0)
    share(0, 3, 0)
    combine(1, 1, 0, 1)
    share(0, 1, 0)
    share(1, 0, 0)
    combine(0, 1, 1, 0)
    combine(0, 1, 0, 1)
    combine(0, 0, 3, 0)
    combine(0, 0, 1, 0)
    share(0, 0, 0)
    combine(1, 0, 0, 0)
    combine(1, 1, 0, 0)
    combine(0, 1, 0, 0)
    combine(0, 0, 0, 0)
    for copy in sent:
        copy.wait_send()
    for copy in ended:
        copy.wait()


def local(sections, block_input, incoming, in_weight, short_taps, medium_taps, skip_weight):
    _, micro, length, width = block_input.shape
    model_width = in_weight.shape[1]
    lags = short_taps.shape[1]
    groups = medium_taps.shape[2]
    weights = jnp.transpose(in_weight, (0, 2, 1, 3))
    taps = jnp.transpose(short_taps, (1, 2, 0, 3)).reshape(lags * 3, 1, width)
    medium = jnp.transpose(medium_taps, (0, 2, 1))
    parts = 3 * (width // 128)
    anywhere = pl.BlockSpec(memory_space=pl.ANY)
    dma = pltpu.SemaphoreType.DMA
    return pl.pallas_call(
        functools.partial(kernel, sections),
        out_shape=jax.ShapeDtypeStruct(block_input.shape, BF16),
        in_specs=[anywhere] * 6,
        out_specs=anywhere,
        scratch_shapes=[
            pltpu.VMEM((micro, 2, 8, length, HALF), BF16),
            pltpu.VMEM((micro, length, width), BF16),
            pltpu.VMEM((3, model_width, width), BF16),
            pltpu.VMEM((lags * 3, 1, width), F32),
            pltpu.VMEM((groups, 128), F32),
            pltpu.VMEM((groups, 128), F32),
            pltpu.VMEM((1, width), F32),
            pltpu.VMEM((micro, parts, length + PAD, 128), F32),
            pltpu.VMEM((parts, length + PAD, 128), F32),
            pltpu.VMEM((micro, 3 * width, length), BF16),
            pltpu.VMEM((groups * 128, 256), BF16),
            pltpu.VMEM((groups * 128, 256), BF16),
            pltpu.VMEM((micro, 2, 8, HALF, length), F32),
            pltpu.VMEM((micro, 2, 8, HALF, length), BF16),
            pltpu.VMEM((micro, 2, 8, HALF, length), BF16),
            pltpu.VMEM((micro, 2, length, HALF), BF16),
            dma((8,)),
            dma((8,)),
            dma((micro, 2, 8)),
            dma((micro, 2, 8)),
            dma((micro, 2, 8)),
            dma((micro, 2, 8)),
            dma((micro, 2)),
            dma((micro, 2)),
        ],
        compiler_params=pltpu.CompilerParams(
            collective_id=0, has_side_effects=True, vmem_limit_bytes=56 * 1024 * 1024
        ),
    )(block_input, incoming, weights, taps, medium, skip_weight)


def solution(mesh):
    in_specs = (
        P("section", None, None, "tp"),
        P("section", None, None, "tp"),
        P("section", None, None, "tp"),
        P("section", None, None, "tp"),
        P("section", None, "tp"),
        P("section", "tp"),
    )
    out_specs = P("section", None, None, "tp")
    return jax.shard_map(
        functools.partial(local, mesh.shape["section"]),
        mesh=mesh, in_specs=in_specs, out_specs=out_specs, check_vma=False,
    )
```

```python
import functools

import jax
import jax.numpy as jnp
from jax import lax
from jax.experimental import pallas as pl
from jax.experimental.pallas import tpu as pltpu
from jax.sharding import PartitionSpec as P

MESH = pl.DeviceIdType.MESH
F32 = jnp.float32
BF16 = jnp.bfloat16
PAD = 8
HALF = 256
RIGHT, LEFT, ACROSS = (1, 0), (3, 0), (0, 1)

ORIGIN = {
    0: [(RIGHT, (1, 0)), (LEFT, (3, 0)), (ACROSS, (0, 1))],
    1: [(ACROSS, (0, 1)), (RIGHT, (1, 0)), (LEFT, (3, 0))],
}


def forwards(mb, cls, key):
    if cls == 0:
        far = RIGHT if mb == 0 else LEFT
        table = {
            (1, 0): [(ACROSS, (1, 1))],
            (3, 0): [(ACROSS, (3, 1))],
            (2, 0): [(ACROSS, (2, 1))],
        }
        table[far].insert(0, (far, (2, 0)))
    else:
        table = {
            (0, 1): [(RIGHT, (1, 1)), (LEFT, (3, 1))],
            (1, 0): [(RIGHT, (2, 0))],
            (3, 1): [(LEFT, (2, 1))],
        }
    return table.get(key, [])


def returns(mb, cls, key):
    if cls == 0:
        far = RIGHT if mb == 0 else LEFT
        if key[1] == 1:
            return ACROSS, []
        if key == (2, 0):
            return far, [(2, 1)]
        if key == (0, 0):
            return None, [(0, 1), (1, 0), (3, 0)]
        return key, [(key[0], 1)] + ([(2, 0)] if key == far else [])
    return {
        (2, 0): (RIGHT, []),
        (2, 1): (LEFT, []),
        (1, 1): (RIGHT, []),
        (3, 0): (LEFT, []),
        (1, 0): (RIGHT, [(2, 0)]),
        (3, 1): (LEFT, [(2, 1)]),
        (0, 1): (ACROSS, [(1, 1), (3, 1)]),
        (0, 0): (None, [(3, 0), (1, 0), (0, 1)]),
    }[key]


def slot(key):
    return key[0] * 2 + key[1]


def split_two(value):
    high = value.astype(BF16)
    low = (value - high.astype(F32)).astype(BF16)
    return high, low


def kernel(
    sections, x_hbm, inc_hbm, w_hbm, taps_hbm, medium_hbm, skip_hbm, out_hbm,
    xbuf, inc, w, taps, medium, flipped, skip, proj, turn, grad_t, fwd_t, bwd_t, partial, sendbuf, recvbuf, final,
    local_sem, w_sem, ag_send, ag_recv, rs_send, rs_recv, fin_send, fin_recv,
):
    me = lax.axis_index("tp")
    sec = lax.axis_index("section")
    below = lax.rem(sec + sections - 1, sections)
    above = lax.rem(sec + 1, sections)
    micro, length, width = inc.shape
    blocks = width // 128
    column, row = lax.div(me, 2), lax.rem(me, 2)

    def device_at(dx, dy):
        return lax.rem(column + 4 + dx, 4) * 2 + lax.rem(row + dy, 2)

    def rows_of(device, start, size):
        return pl.ds(pl.multiple_of(device * width + start, HALF), size)

    small = [
        pltpu.make_async_copy(medium_hbm.at[0], medium, local_sem.at[0]),
        pltpu.make_async_copy(taps_hbm, taps, local_sem.at[1]),
        pltpu.make_async_copy(skip_hbm, skip, local_sem.at[2]),
        pltpu.make_async_copy(inc_hbm.at[0], inc, local_sem.at[3]),
    ]
    own_x = [
        [
            pltpu.make_async_copy(
                x_hbm.at[0, mb, :, pl.ds(cls * HALF, HALF)], xbuf.at[mb, cls, 0], local_sem.at[4 + mb * 2 + cls]
            )
            for cls in range(2)
        ]
        for mb in range(micro)
    ]

    def w_copy(key):
        rows = rows_of(device_at(-key[0], key[1]), 0, width)
        return pltpu.make_async_copy(w_hbm.at[0, :, rows, :], w.at[:, rows, :], w_sem.at[slot(key)])

    barrier = pltpu.get_barrier_semaphore()
    for hop in (RIGHT, LEFT, ACROSS):
        pl.semaphore_signal(barrier, inc=1, device_id={"tp": device_at(*hop)}, device_id_type=MESH)
    pl.semaphore_signal(barrier, inc=1, device_id={"section": below}, device_id_type=MESH)
    pl.semaphore_signal(barrier, inc=1, device_id={"section": above}, device_id_type=MESH)
    for mb in range(micro):
        for cls in range(2):
            own_x[mb][cls].start()
    small[0].start()
    arrival = [(0, 0), (3, 1), (1, 0), (3, 0), (0, 1), (1, 1), (2, 0), (2, 1)]
    for key in arrival:
        w_copy(key).start()
    for copy in small[1:]:
        copy.start()

    place_r = lax.broadcasted_iota(jnp.int32, (128, 128), 0)
    place_c = lax.broadcasted_iota(jnp.int32, (128, 128), 1)
    small[0].wait()
    flip = jnp.where(lax.rem(place_r + place_c, 128) == 0, 1.0, 0.0).astype(F32)
    flipped[...] = jnp.dot(medium[...], flip, precision=lax.Precision.HIGHEST, preferred_element_type=F32)
    for part in range(3 * blocks):
        for mb in range(micro):
            proj[mb, part, 0:PAD, :] = jnp.zeros((PAD, 128), F32)
        turn[part, length : length + PAD, :] = jnp.zeros((PAD, 128), F32)
    for mb in range(micro):
        for cls in range(2):
            own_x[mb][cls].wait()

    pl.semaphore_wait(barrier, 5)

    sent = []

    def gather_copy(mb, cls, source, hop, key):
        return pltpu.make_async_remote_copy(
            src_ref=xbuf.at[mb, cls, slot(source)],
            dst_ref=xbuf.at[mb, cls, slot(key)],
            send_sem=ag_send.at[mb, cls, slot(key)],
            recv_sem=ag_recv.at[mb, cls, slot(key)],
            device_id={"tp": device_at(*hop)},
            device_id_type=MESH,
        )

    def origin(mb, cls, number):
        hop, key = ORIGIN[cls][number]
        copy = gather_copy(mb, cls, (0, 0), hop, key)
        copy.start()
        sent.append(copy)

    def handle(mb, cls, dx, dy):
        gather_copy(mb, cls, (0, 0), RIGHT, (dx, dy)).wait_recv()
        for hop, there in forwards(mb, cls, (dx, dy)):
            copy = gather_copy(mb, cls, (dx, dy), hop, there)
            copy.start()
            sent.append(copy)

    loaded, begun = set(), set()

    def project(mb, dx, dy):
        if (dx, dy) not in loaded:
            w_copy((dx, dy)).wait()
            loaded.add((dx, dy))
        rows = rows_of(device_at(-dx, dy), 0, width)
        chunk = jnp.concatenate([xbuf[mb, 0, slot((dx, dy))], xbuf[mb, 1, slot((dx, dy))]], axis=1)
        for stream in range(3):
            total = jnp.dot(chunk, w[stream, rows, :], preferred_element_type=F32)
            for block in range(blocks):
                piece = total[:, block * 128 : block * 128 + 128]
                where = (mb, stream * blocks + block, pl.ds(PAD, length), slice(None))
                proj[where] = proj[where] + piece if mb in begun else piece
        begun.add(mb)

    def build_tables(number):
        for group in range(4 * number, 4 * number + 4):
            rows = pl.ds(group * 128, 128)
            ahead = jnp.broadcast_to(medium[pl.ds(group, 1), :], (128, 128))
            ahead = pltpu.roll(ahead, 0, 1, stride=1, stride_axis=0)
            high, low = split_two(jnp.where(place_c >= place_r, ahead, 0.0))
            bwd_t[rows, 0:128] = high
            bwd_t[rows, 128:256] = low
            behind = jnp.broadcast_to(flipped[pl.ds(group, 1), :], (128, 128))
            behind = pltpu.roll(behind, 0, 1, stride=1, stride_axis=0)
            high, low = split_two(jnp.where(place_c <= place_r, behind, 0.0))
            fwd_t[rows, 0:128] = high
            fwd_t[rows, 128:256] = low

    def medium_conv(table, block, value):
        high, low = split_two(value)
        both = jnp.concatenate([high, low], axis=1)
        both = jnp.concatenate([both, both], axis=0)
        rows = pl.ds(block * 1024, 1024)
        raw = jnp.dot(table[rows, :], both, preferred_element_type=F32)
        lane_group = lax.div(place_c, 16)
        total = raw[0:length, 0:128] + raw[0:length, 128:256]
        for group in range(1, 8):
            first = group * 128
            piece = raw[first : first + length, 0:128] + raw[first : first + length, 128:256]
            total = jnp.where(lane_group == group, piece, total)
        return total

    ready = []

    def mixer(mb, half):
        while len(ready) < len(small) - 1:
            ready.append(small[len(ready) + 1].wait())

        def one_block(block):
            lanes = pl.ds(block * 128, 128)

            def featured(stream):
                total = jnp.zeros((length, 128), F32)
                for lag in range(7):
                    tap = taps[lag * 3 + stream, :, lanes]
                    total = total + tap * proj[mb, stream * blocks + block, pl.ds(PAD - lag, length), :]
                return total

            query, key, value = featured(0), featured(1), featured(2)
            gain = skip[:, lanes]
            product = key * value
            mixed = medium_conv(fwd_t, block, product) + gain * product
            upstream = inc[mb, :, lanes].astype(F32)
            mixed_grad = upstream * query
            product_grad = medium_conv(bwd_t, block, mixed_grad) + gain * mixed_grad
            turn[block, 0:length, :] = upstream * mixed
            turn[blocks + block, 0:length, :] = product_grad * value
            turn[2 * blocks + block, 0:length, :] = product_grad * key
            for stream in range(3):
                total = jnp.zeros((length, 128), F32)
                for lag in range(7):
                    tap = taps[lag * 3 + stream, :, lanes]
                    total = total + tap * turn[stream * blocks + block, pl.ds(lag, length), :]
                rows = pl.ds(stream * width + block * 128, 128)
                grad_t[mb, rows, :] = jnp.transpose(total).astype(BF16)

        for block in range(2 * half, 2 * half + 2):
            one_block(block)

    def sum_copy(mb, cls, key, hop):
        return pltpu.make_async_remote_copy(
            src_ref=sendbuf.at[mb, cls, slot(key)],
            dst_ref=recvbuf.at[mb, cls, slot(key)],
            send_sem=rs_send.at[mb, cls, slot(key)],
            recv_sem=rs_recv.at[mb, cls, slot(key)],
            device_id={"tp": device_at(*hop)},
            device_id_type=MESH,
        )

    def push_sum(mb, cls, key, hop, value):
        sendbuf[mb, cls, slot(key)] = value.astype(BF16)
        copy = sum_copy(mb, cls, key, hop)
        copy.start()
        sent.append(copy)

    def share(mb, dx, dy):
        key = (dx, dy)
        rows = rows_of(device_at(*key), 0, width)
        total = None
        for stream in range(3):
            part = jnp.dot(
                w[stream, rows, :], grad_t[mb, stream * width : stream * width + width, :], preferred_element_type=F32
            )
            total = part if total is None else total + part
        for cls in range(2):
            piece = total[cls * HALF : cls * HALF + HALF, :]
            hop, joins = returns(mb, cls, key)
            if hop is not None and not joins:
                push_sum(mb, cls, key, hop, piece)
            else:
                partial[mb, cls, slot(key)] = piece

    def combine(mb, cls, dx, dy):
        key = (dx, dy)
        hop, joins = returns(mb, cls, key)
        total = partial[mb, cls, slot(key)]
        for join in joins:
            sum_copy(mb, cls, join, RIGHT).wait_recv()
            total = total + recvbuf[mb, cls, slot(join)].astype(F32)
        if hop is not None:
            push_sum(mb, cls, key, hop, total)
            return
        upstream = inc[mb, :, cls * HALF : cls * HALF + HALF].astype(F32)
        final[mb, cls] = (jnp.transpose(total) + upstream).astype(BF16)
        copy = pltpu.make_async_remote_copy(
            src_ref=final.at[mb, cls],
            dst_ref=out_hbm.at[0, mb, :, pl.ds(cls * HALF, HALF)],
            send_sem=fin_send.at[mb, cls],
            recv_sem=fin_recv.at[mb, cls],
            device_id={"section": below},
            device_id_type=MESH,
        )
        copy.start()
        ended.append(copy)

    ended = []
    origin(0, 0, 1)
    origin(0, 1, 0)
    origin(1, 0, 1)
    origin(0, 0, 0)
    origin(0, 1, 1)
    origin(1, 1, 2)
    project(0, 0, 0)
    origin(0, 1, 2)
    origin(1, 1, 1)
    origin(0, 0, 2)
    origin(1, 1, 0)
    build_tables(5)
    build_tables(2)
    project(1, 0, 0)
    build_tables(6)
    build_tables(4)
    build_tables(0)
    handle(0, 0, 3, 0)
    handle(0, 0, 1, 0)
    handle(0, 1, 0, 1)
    build_tables(7)
    origin(1, 0, 2)
    origin(1, 0, 0)
    handle(0, 0, 0, 1)
    handle(0, 1, 1, 0)
    handle(1, 0, 3, 0)
    build_tables(1)
    handle(1, 1, 0, 1)
    handle(0, 0, 3, 1)
    handle(1, 1, 3, 0)
    project(1, 3, 0)
    handle(0, 0, 2, 0)
    handle(0, 1, 3, 1)
    project(0, 3, 1)
    handle(0, 0, 1, 1)
    handle(1, 1, 1, 0)
    build_tables(3)
    handle(0, 1, 3, 0)
    project(0, 1, 0)
    project(0, 3, 0)
    handle(1, 0, 0, 1)
    handle(1, 0, 2, 0)
    project(1, 0, 1)
    handle(0, 1, 1, 1)
    project(0, 0, 1)
    project(0, 1, 1)
    handle(1, 1, 3, 1)
    handle(1, 0, 1, 0)
    handle(0, 1, 2, 0)
    handle(1, 0, 3, 1)
    project(1, 3, 1)
    project(1, 1, 0)
    project(0, 2, 0)
    handle(0, 1, 2, 1)
    handle(0, 0, 2, 1)
    project(0, 2, 1)
    mixer(0, 1)
    mixer(0, 0)
    share(0, 1, 1)
    share(0, 2, 1)
    handle(1, 1, 2, 1)
    handle(1, 1, 2, 0)
    handle(1, 0, 2, 1)
    project(1, 2, 0)
    handle(1, 0, 1, 1)
    handle(1, 1, 1, 1)
    project(1, 2, 1)
    project(1, 1, 1)
    mixer(1, 0)
    mixer(1, 1)
    share(1, 2, 1)
    share(0, 2, 0)
    share(1, 3, 1)
    share(0, 3, 1)
    combine(0, 1, 3, 1)
    combine(0, 0, 2, 0)
    share(1, 3, 0)
    share(1, 2, 0)
    share(0, 1, 0)
    share(1, 1, 1)
    combine(1, 1, 3, 1)
    share(0, 0, 1)
    combine(1, 0, 2, 0)
    combine(0, 1, 1, 0)
    combine(0, 1, 0, 1)
    share(1, 0, 1)
    share(0, 3, 0)
    share(1, 1, 0)
    combine(0, 0, 1, 0)
    combine(0, 0, 3, 0)
    share(0, 0, 0)
    share(1, 0, 0)
    combine(1, 1, 1, 0)
    combine(1, 1, 0, 1)
    combine(1, 0, 1, 0)
    combine(1, 0, 3, 0)
    combine(0, 1, 0, 0)
    combine(0, 0, 0, 0)
    combine(1, 1, 0, 0)
    combine(1, 0, 0, 0)
    for copy in sent:
        copy.wait_send()
    for copy in ended:
        copy.wait()


def local(sections, block_input, incoming, in_weight, short_taps, medium_taps, skip_weight):
    _, micro, length, width = block_input.shape
    model_width = in_weight.shape[1]
    lags = short_taps.shape[1]
    groups = medium_taps.shape[2]
    weights = jnp.transpose(in_weight, (0, 2, 1, 3))
    taps = jnp.transpose(short_taps, (1, 2, 0, 3)).reshape(lags * 3, 1, width)
    medium = jnp.transpose(medium_taps, (0, 2, 1))
    parts = 3 * (width // 128)
    anywhere = pl.BlockSpec(memory_space=pl.ANY)
    dma = pltpu.SemaphoreType.DMA
    return pl.pallas_call(
        functools.partial(kernel, sections),
        out_shape=jax.ShapeDtypeStruct(block_input.shape, BF16),
        in_specs=[anywhere] * 6,
        out_specs=anywhere,
        scratch_shapes=[
            pltpu.VMEM((micro, 2, 8, length, HALF), BF16),
            pltpu.VMEM((micro, length, width), BF16),
            pltpu.VMEM((3, model_width, width), BF16),
            pltpu.VMEM((lags * 3, 1, width), F32),
            pltpu.VMEM((groups, 128), F32),
            pltpu.VMEM((groups, 128), F32),
            pltpu.VMEM((1, width), F32),
            pltpu.VMEM((micro, parts, length + PAD, 128), F32),
            pltpu.VMEM((parts, length + PAD, 128), F32),
            pltpu.VMEM((micro, 3 * width, length), BF16),
            pltpu.VMEM((groups * 128, 256), BF16),
            pltpu.VMEM((groups * 128, 256), BF16),
            pltpu.VMEM((micro, 2, 8, HALF, length), F32),
            pltpu.VMEM((micro, 2, 8, HALF, length), BF16),
            pltpu.VMEM((micro, 2, 8, HALF, length), BF16),
            pltpu.VMEM((micro, 2, length, HALF), BF16),
            dma((8,)),
            dma((8,)),
            dma((micro, 2, 8)),
            dma((micro, 2, 8)),
            dma((micro, 2, 8)),
            dma((micro, 2, 8)),
            dma((micro, 2)),
            dma((micro, 2)),
        ],
        compiler_params=pltpu.CompilerParams(
            collective_id=0, has_side_effects=True, vmem_limit_bytes=56 * 1024 * 1024
        ),
    )(block_input, incoming, weights, taps, medium, skip_weight)


def solution(mesh):
    in_specs = (
        P("section", None, None, "tp"),
        P("section", None, None, "tp"),
        P("section", None, None, "tp"),
        P("section", None, None, "tp"),
        P("section", None, "tp"),
        P("section", "tp"),
    )
    out_specs = P("section", None, None, "tp")
    return jax.shard_map(
        functools.partial(local, mesh.shape["section"]),
        mesh=mesh, in_specs=in_specs, out_specs=out_specs, check_vma=False,
    )
```

```python
import functools

import jax
import jax.numpy as jnp
from jax import lax
from jax.experimental import pallas as pl
from jax.experimental.pallas import tpu as pltpu
from jax.sharding import PartitionSpec as P

MESH = pl.DeviceIdType.MESH
F32 = jnp.float32
BF16 = jnp.bfloat16
PAD = 8
HALF = 256
RIGHT, LEFT, ACROSS = (1, 0), (3, 0), (0, 1)

ORIGIN = {
    0: [(RIGHT, (1, 0)), (LEFT, (3, 0)), (ACROSS, (0, 1))],
    1: [(ACROSS, (0, 1)), (RIGHT, (1, 0)), (LEFT, (3, 0))],
}


def forwards(mb, cls, key):
    if cls == 0:
        far = RIGHT if mb == 0 else LEFT
        table = {
            (1, 0): [(ACROSS, (1, 1))],
            (3, 0): [(ACROSS, (3, 1))],
            (2, 0): [(ACROSS, (2, 1))],
        }
        table[far].insert(0, (far, (2, 0)))
    else:
        table = {
            (0, 1): [(RIGHT, (1, 1)), (LEFT, (3, 1))],
            (1, 0): [(RIGHT, (2, 0))],
            (3, 1): [(LEFT, (2, 1))],
        }
    return table.get(key, [])


def returns(mb, cls, key):
    if cls == 0:
        far = RIGHT if mb == 0 else LEFT
        if key[1] == 1:
            return ACROSS, []
        if key == (2, 0):
            return far, [(2, 1)]
        if key == (0, 0):
            return None, [(0, 1), (1, 0), (3, 0)]
        return key, [(key[0], 1)] + ([(2, 0)] if key == far else [])
    return {
        (2, 0): (RIGHT, []),
        (2, 1): (LEFT, []),
        (1, 1): (RIGHT, []),
        (3, 0): (LEFT, []),
        (1, 0): (RIGHT, [(2, 0)]),
        (3, 1): (LEFT, [(2, 1)]),
        (0, 1): (ACROSS, [(1, 1), (3, 1)]),
        (0, 0): (None, [(3, 0), (1, 0), (0, 1)]),
    }[key]


def slot(key):
    return key[0] * 2 + key[1]


def split_two(value):
    high = value.astype(BF16)
    low = (value - high.astype(F32)).astype(BF16)
    return high, low


def kernel(
    sections, x_hbm, inc_hbm, w_hbm, taps_hbm, medium_hbm, skip_hbm, out_hbm,
    xbuf, inc, w, taps, medium, flipped, skip, proj, turn, grad_t, fwd_t, bwd_t, partial, sendbuf, recvbuf, final,
    local_sem, w_sem, ag_send, ag_recv, rs_send, rs_recv, fin_send, fin_recv,
):
    me = lax.axis_index("tp")
    sec = lax.axis_index("section")
    below = lax.rem(sec + sections - 1, sections)
    above = lax.rem(sec + 1, sections)
    micro, length, width = inc.shape
    blocks = width // 128
    column, row = lax.div(me, 2), lax.rem(me, 2)

    def device_at(dx, dy):
        return lax.rem(column + 4 + dx, 4) * 2 + lax.rem(row + dy, 2)

    def rows_of(device, start, size):
        return pl.ds(pl.multiple_of(device * width + start, HALF), size)

    small = [
        pltpu.make_async_copy(medium_hbm.at[0], medium, local_sem.at[0]),
        pltpu.make_async_copy(taps_hbm, taps, local_sem.at[1]),
        pltpu.make_async_copy(skip_hbm, skip, local_sem.at[2]),
        pltpu.make_async_copy(inc_hbm.at[0], inc, local_sem.at[3]),
    ]
    own_x = [
        [
            pltpu.make_async_copy(
                x_hbm.at[0, mb, :, pl.ds(cls * HALF, HALF)], xbuf.at[mb, cls, 0], local_sem.at[4 + mb * 2 + cls]
            )
            for cls in range(2)
        ]
        for mb in range(micro)
    ]

    def w_copy(key):
        rows = rows_of(device_at(-key[0], key[1]), 0, width)
        return pltpu.make_async_copy(w_hbm.at[0, :, rows, :], w.at[:, rows, :], w_sem.at[slot(key)])

    barrier = pltpu.get_barrier_semaphore()
    for hop in (RIGHT, LEFT, ACROSS):
        pl.semaphore_signal(barrier, inc=1, device_id={"tp": device_at(*hop)}, device_id_type=MESH)
    pl.semaphore_signal(barrier, inc=1, device_id={"section": below}, device_id_type=MESH)
    pl.semaphore_signal(barrier, inc=1, device_id={"section": above}, device_id_type=MESH)
    for mb in range(micro):
        for cls in range(2):
            own_x[mb][cls].start()
    small[0].start()
    arrival = [(0, 0), (3, 1), (1, 0), (3, 0), (0, 1), (1, 1), (2, 0), (2, 1)]
    for key in arrival:
        w_copy(key).start()
    for copy in small[1:]:
        copy.start()

    place_r = lax.broadcasted_iota(jnp.int32, (128, 128), 0)
    place_c = lax.broadcasted_iota(jnp.int32, (128, 128), 1)
    small[0].wait()
    flip = jnp.where(lax.rem(place_r + place_c, 128) == 0, 1.0, 0.0).astype(F32)
    flipped[...] = jnp.dot(medium[...], flip, precision=lax.Precision.HIGHEST, preferred_element_type=F32)
    for part in range(3 * blocks):
        for mb in range(micro):
            proj[mb, part, 0:PAD, :] = jnp.zeros((PAD, 128), F32)
        turn[part, length : length + PAD, :] = jnp.zeros((PAD, 128), F32)
    for mb in range(micro):
        for cls in range(2):
            own_x[mb][cls].wait()

    pl.semaphore_wait(barrier, 5)

    sent = []

    def gather_copy(mb, cls, source, hop, key):
        return pltpu.make_async_remote_copy(
            src_ref=xbuf.at[mb, cls, slot(source)],
            dst_ref=xbuf.at[mb, cls, slot(key)],
            send_sem=ag_send.at[mb, cls, slot(key)],
            recv_sem=ag_recv.at[mb, cls, slot(key)],
            device_id={"tp": device_at(*hop)},
            device_id_type=MESH,
        )

    def origin(mb, cls, number):
        hop, key = ORIGIN[cls][number]
        copy = gather_copy(mb, cls, (0, 0), hop, key)
        copy.start()
        sent.append(copy)

    def handle(mb, cls, dx, dy):
        gather_copy(mb, cls, (0, 0), RIGHT, (dx, dy)).wait_recv()
        for hop, there in forwards(mb, cls, (dx, dy)):
            copy = gather_copy(mb, cls, (dx, dy), hop, there)
            copy.start()
            sent.append(copy)

    loaded, begun = set(), set()

    def project(mb, dx, dy):
        if (dx, dy) not in loaded:
            w_copy((dx, dy)).wait()
            loaded.add((dx, dy))
        rows = rows_of(device_at(-dx, dy), 0, width)
        chunk = jnp.concatenate([xbuf[mb, 0, slot((dx, dy))], xbuf[mb, 1, slot((dx, dy))]], axis=1)
        for stream in range(3):
            total = jnp.dot(chunk, w[stream, rows, :], preferred_element_type=F32)
            for block in range(blocks):
                piece = total[:, block * 128 : block * 128 + 128]
                where = (mb, stream * blocks + block, pl.ds(PAD, length), slice(None))
                proj[where] = proj[where] + piece if mb in begun else piece
        begun.add(mb)

    def build_tables(number):
        for group in range(4 * number, 4 * number + 4):
            rows = pl.ds(group * 128, 128)
            ahead = jnp.broadcast_to(medium[pl.ds(group, 1), :], (128, 128))
            ahead = pltpu.roll(ahead, 0, 1, stride=1, stride_axis=0)
            high, low = split_two(jnp.where(place_c >= place_r, ahead, 0.0))
            bwd_t[rows, 0:128] = high
            bwd_t[rows, 128:256] = low
            behind = jnp.broadcast_to(flipped[pl.ds(group, 1), :], (128, 128))
            behind = pltpu.roll(behind, 0, 1, stride=1, stride_axis=0)
            high, low = split_two(jnp.where(place_c <= place_r, behind, 0.0))
            fwd_t[rows, 0:128] = high
            fwd_t[rows, 128:256] = low

    def medium_conv(table, block, value):
        high, low = split_two(value)
        both = jnp.concatenate([high, low], axis=1)
        both = jnp.concatenate([both, both], axis=0)
        rows = pl.ds(block * 1024, 1024)
        raw = jnp.dot(table[rows, :], both, preferred_element_type=F32)
        lane_group = lax.div(place_c, 16)
        total = raw[0:length, 0:128] + raw[0:length, 128:256]
        for group in range(1, 8):
            first = group * 128
            piece = raw[first : first + length, 0:128] + raw[first : first + length, 128:256]
            total = jnp.where(lane_group == group, piece, total)
        return total

    ready = []

    def mixer(mb, half):
        while len(ready) < len(small) - 1:
            ready.append(small[len(ready) + 1].wait())

        def one_block(block):
            lanes = pl.ds(block * 128, 128)

            def featured(stream):
                total = jnp.zeros((length, 128), F32)
                for lag in range(7):
                    tap = taps[lag * 3 + stream, :, lanes]
                    total = total + tap * proj[mb, stream * blocks + block, pl.ds(PAD - lag, length), :]
                return total

            query, key, value = featured(0), featured(1), featured(2)
            gain = skip[:, lanes]
            product = key * value
            mixed = medium_conv(fwd_t, block, product) + gain * product
            upstream = inc[mb, :, lanes].astype(F32)
            mixed_grad = upstream * query
            product_grad = medium_conv(bwd_t, block, mixed_grad) + gain * mixed_grad
            turn[block, 0:length, :] = upstream * mixed
            turn[blocks + block, 0:length, :] = product_grad * value
            turn[2 * blocks + block, 0:length, :] = product_grad * key
            for stream in range(3):
                total = jnp.zeros((length, 128), F32)
                for lag in range(7):
                    tap = taps[lag * 3 + stream, :, lanes]
                    total = total + tap * turn[stream * blocks + block, pl.ds(lag, length), :]
                rows = pl.ds(stream * width + block * 128, 128)
                grad_t[mb, rows, :] = jnp.transpose(total).astype(BF16)

        for block in range(2 * half, 2 * half + 2):
            one_block(block)

    def sum_copy(mb, cls, key, hop):
        return pltpu.make_async_remote_copy(
            src_ref=sendbuf.at[mb, cls, slot(key)],
            dst_ref=recvbuf.at[mb, cls, slot(key)],
            send_sem=rs_send.at[mb, cls, slot(key)],
            recv_sem=rs_recv.at[mb, cls, slot(key)],
            device_id={"tp": device_at(*hop)},
            device_id_type=MESH,
        )

    def push_sum(mb, cls, key, hop, value):
        sendbuf[mb, cls, slot(key)] = value.astype(BF16)
        copy = sum_copy(mb, cls, key, hop)
        copy.start()
        sent.append(copy)

    def share(mb, dx, dy):
        key = (dx, dy)
        rows = rows_of(device_at(*key), 0, width)
        total = None
        for stream in range(3):
            part = jnp.dot(
                w[stream, rows, :], grad_t[mb, stream * width : stream * width + width, :], preferred_element_type=F32
            )
            total = part if total is None else total + part
        for cls in range(2):
            piece = total[cls * HALF : cls * HALF + HALF, :]
            hop, joins = returns(mb, cls, key)
            if hop is not None and not joins:
                push_sum(mb, cls, key, hop, piece)
            else:
                partial[mb, cls, slot(key)] = piece

    def combine(mb, cls, dx, dy):
        key = (dx, dy)
        hop, joins = returns(mb, cls, key)
        total = partial[mb, cls, slot(key)]
        for join in joins:
            sum_copy(mb, cls, join, RIGHT).wait_recv()
            total = total + recvbuf[mb, cls, slot(join)].astype(F32)
        if hop is not None:
            push_sum(mb, cls, key, hop, total)
            return
        upstream = inc[mb, :, cls * HALF : cls * HALF + HALF].astype(F32)
        final[mb, cls] = (jnp.transpose(total) + upstream).astype(BF16)
        copy = pltpu.make_async_remote_copy(
            src_ref=final.at[mb, cls],
            dst_ref=out_hbm.at[0, mb, :, pl.ds(cls * HALF, HALF)],
            send_sem=fin_send.at[mb, cls],
            recv_sem=fin_recv.at[mb, cls],
            device_id={"section": below},
            device_id_type=MESH,
        )
        copy.start()
        ended.append(copy)

    ended = []
    origin(0, 0, 1)
    origin(0, 1, 0)
    origin(1, 0, 1)
    origin(0, 0, 0)
    origin(0, 1, 1)
    origin(1, 1, 2)
    project(0, 0, 0)
    origin(0, 1, 2)
    origin(1, 1, 1)
    origin(0, 0, 2)
    origin(1, 1, 0)
    build_tables(5)
    build_tables(2)
    project(1, 0, 0)
    build_tables(6)
    build_tables(4)
    build_tables(0)
    handle(0, 0, 3, 0)
    handle(0, 0, 1, 0)
    handle(0, 1, 0, 1)
    build_tables(7)
    origin(1, 0, 2)
    origin(1, 0, 0)
    handle(0, 0, 0, 1)
    handle(0, 1, 1, 0)
    handle(1, 0, 3, 0)
    build_tables(1)
    handle(1, 1, 0, 1)
    handle(0, 0, 3, 1)
    handle(1, 1, 3, 0)
    project(1, 3, 0)
    handle(0, 0, 2, 0)
    handle(0, 1, 3, 1)
    project(0, 3, 1)
    handle(0, 0, 1, 1)
    handle(1, 1, 1, 0)
    build_tables(3)
    handle(0, 1, 3, 0)
    project(0, 1, 0)
    project(0, 3, 0)
    handle(1, 0, 0, 1)
    handle(1, 0, 2, 0)
    project(1, 0, 1)
    handle(0, 1, 1, 1)
    project(0, 0, 1)
    project(0, 1, 1)
    handle(1, 1, 3, 1)
    handle(1, 0, 1, 0)
    handle(0, 1, 2, 0)
    handle(1, 0, 3, 1)
    project(1, 3, 1)
    project(1, 1, 0)
    project(0, 2, 0)
    handle(0, 1, 2, 1)
    handle(0, 0, 2, 1)
    project(0, 2, 1)
    mixer(0, 1)
    mixer(0, 0)
    share(0, 1, 1)
    share(0, 2, 1)
    handle(1, 1, 2, 1)
    handle(1, 1, 2, 0)
    handle(1, 0, 2, 1)
    project(1, 2, 0)
    handle(1, 0, 1, 1)
    handle(1, 1, 1, 1)
    project(1, 2, 1)
    project(1, 1, 1)
    mixer(1, 0)
    mixer(1, 1)
    share(1, 2, 1)
    share(0, 2, 0)
    share(1, 3, 1)
    share(0, 3, 1)
    combine(0, 1, 3, 1)
    combine(0, 0, 2, 0)
    share(1, 3, 0)
    share(1, 2, 0)
    share(0, 1, 0)
    share(1, 1, 1)
    combine(1, 1, 3, 1)
    share(0, 0, 1)
    combine(1, 0, 2, 0)
    combine(0, 1, 1, 0)
    combine(0, 1, 0, 1)
    share(1, 0, 1)
    share(0, 3, 0)
    share(1, 1, 0)
    combine(0, 0, 1, 0)
    combine(0, 0, 3, 0)
    share(0, 0, 0)
    share(1, 0, 0)
    combine(1, 1, 1, 0)
    combine(1, 1, 0, 1)
    combine(1, 0, 1, 0)
    combine(1, 0, 3, 0)
    combine(0, 1, 0, 0)
    combine(0, 0, 0, 0)
    combine(1, 1, 0, 0)
    combine(1, 0, 0, 0)
    for copy in sent:
        copy.wait_send()
    for copy in ended:
        copy.wait()


def local(sections, block_input, incoming, in_weight, short_taps, medium_taps, skip_weight):
    _, micro, length, width = block_input.shape
    model_width = in_weight.shape[1]
    lags = short_taps.shape[1]
    groups = medium_taps.shape[2]
    weights = jnp.transpose(in_weight, (0, 2, 1, 3))
    taps = jnp.transpose(short_taps, (1, 2, 0, 3)).reshape(lags * 3, 1, width)
    medium = jnp.transpose(medium_taps, (0, 2, 1))
    parts = 3 * (width // 128)
    block_input, incoming, taps, medium, skip_weight = (
        pltpu.with_memory_space_constraint(value, pltpu.HBM)
        for value in (block_input, incoming, taps, medium, skip_weight)
    )
    anywhere = pl.BlockSpec(memory_space=pl.ANY)
    dma = pltpu.SemaphoreType.DMA
    return pl.pallas_call(
        functools.partial(kernel, sections),
        out_shape=jax.ShapeDtypeStruct(block_input.shape, BF16),
        in_specs=[anywhere] * 6,
        out_specs=anywhere,
        scratch_shapes=[
            pltpu.VMEM((micro, 2, 8, length, HALF), BF16),
            pltpu.VMEM((micro, length, width), BF16),
            pltpu.VMEM((3, model_width, width), BF16),
            pltpu.VMEM((lags * 3, 1, width), F32),
            pltpu.VMEM((groups, 128), F32),
            pltpu.VMEM((groups, 128), F32),
            pltpu.VMEM((1, width), F32),
            pltpu.VMEM((micro, parts, length + PAD, 128), F32),
            pltpu.VMEM((parts, length + PAD, 128), F32),
            pltpu.VMEM((micro, 3 * width, length), BF16),
            pltpu.VMEM((groups * 128, 256), BF16),
            pltpu.VMEM((groups * 128, 256), BF16),
            pltpu.VMEM((micro, 2, 8, HALF, length), F32),
            pltpu.VMEM((micro, 2, 8, HALF, length), BF16),
            pltpu.VMEM((micro, 2, 8, HALF, length), BF16),
            pltpu.VMEM((micro, 2, length, HALF), BF16),
            dma((8,)),
            dma((8,)),
            dma((micro, 2, 8)),
            dma((micro, 2, 8)),
            dma((micro, 2, 8)),
            dma((micro, 2, 8)),
            dma((micro, 2)),
            dma((micro, 2)),
        ],
        compiler_params=pltpu.CompilerParams(
            collective_id=0, has_side_effects=True, vmem_limit_bytes=48 * 1024 * 1024
        ),
    )(block_input, incoming, weights, taps, medium, skip_weight)


def solution(mesh):
    in_specs = (
        P("section", None, None, "tp"),
        P("section", None, None, "tp"),
        P("section", None, None, "tp"),
        P("section", None, None, "tp"),
        P("section", None, "tp"),
        P("section", "tp"),
    )
    out_specs = P("section", None, None, "tp")
    return jax.shard_map(
        functools.partial(local, mesh.shape["section"]),
        mesh=mesh, in_specs=in_specs, out_specs=out_specs, check_vma=False,
    )
```

```python
import functools

import jax
import jax.numpy as jnp
from jax import lax
from jax.experimental import pallas as pl
from jax.experimental.pallas import tpu as pltpu
from jax.sharding import PartitionSpec as P

MESH = pl.DeviceIdType.MESH
F32 = jnp.float32
BF16 = jnp.bfloat16
PAD = 8
HALF = 256
RIGHT, LEFT, ACROSS = (1, 0), (3, 0), (0, 1)

ORIGIN = {
    0: [(RIGHT, (1, 0)), (LEFT, (3, 0)), (ACROSS, (0, 1))],
    1: [(ACROSS, (0, 1)), (RIGHT, (1, 0)), (LEFT, (3, 0))],
}


def forwards(mb, cls, key):
    if cls == 0:
        far = RIGHT if mb == 0 else LEFT
        table = {
            (1, 0): [(ACROSS, (1, 1))],
            (3, 0): [(ACROSS, (3, 1))],
            (2, 0): [(ACROSS, (2, 1))],
        }
        table[far].insert(0, (far, (2, 0)))
        if mb == 0:
            del table[(2, 0)]
            table[(3, 1)] = [(LEFT, (2, 1))]
    else:
        table = {
            (0, 1): [(RIGHT, (1, 1)), (LEFT, (3, 1))],
            (1, 0): [(RIGHT, (2, 0))],
            (3, 1): [(LEFT, (2, 1))],
        }
    return table.get(key, [])


def returns(mb, cls, key):
    if cls == 0:
        far = RIGHT if mb == 0 else LEFT
        if mb == 0 and key == (2, 1):
            return RIGHT, []
        if key[1] == 1:
            return ACROSS, [(2, 1)] if mb == 0 and key == (1, 1) else []
        if key == (2, 0):
            return far, [] if mb == 0 else [(2, 1)]
        if key == (0, 0):
            return None, [(0, 1), (1, 0), (3, 0)]
        return key, [(key[0], 1)] + ([(2, 0)] if key == far else [])
    return {
        (2, 0): (RIGHT, []),
        (2, 1): (LEFT, []),
        (1, 1): (RIGHT, []),
        (3, 0): (LEFT, []),
        (1, 0): (RIGHT, [(2, 0)]),
        (3, 1): (LEFT, [(2, 1)]),
        (0, 1): (ACROSS, [(1, 1), (3, 1)]),
        (0, 0): (None, [(3, 0), (1, 0), (0, 1)]),
    }[key]


def slot(key):
    return key[0] * 2 + key[1]


def split_two(value):
    high = value.astype(BF16)
    low = (value - high.astype(F32)).astype(BF16)
    return high, low


def kernel(
    sections, x_hbm, inc_hbm, w_hbm, taps_hbm, medium_hbm, skip_hbm, out_hbm,
    xbuf, inc, w, taps, medium, flipped, skip, proj, turn, grad_t, fwd_t, bwd_t, partial, sendbuf, recvbuf, final,
    local_sem, w_sem, ag_send, ag_recv, rs_send, rs_recv, fin_send, fin_recv,
):
    me = lax.axis_index("tp")
    sec = lax.axis_index("section")
    below = lax.rem(sec + sections - 1, sections)
    above = lax.rem(sec + 1, sections)
    micro, length, width = inc.shape
    blocks = width // 128
    column, row = lax.div(me, 2), lax.rem(me, 2)

    def device_at(dx, dy):
        return lax.rem(column + 4 + dx, 4) * 2 + lax.rem(row + dy, 2)

    def rows_of(device, start, size):
        return pl.ds(pl.multiple_of(device * width + start, HALF), size)

    small = [
        pltpu.make_async_copy(medium_hbm.at[0], medium, local_sem.at[0]),
        pltpu.make_async_copy(taps_hbm, taps, local_sem.at[1]),
        pltpu.make_async_copy(skip_hbm, skip, local_sem.at[2]),
        pltpu.make_async_copy(inc_hbm.at[0], inc, local_sem.at[3]),
    ]
    own_x = [
        [
            pltpu.make_async_copy(
                x_hbm.at[0, mb, :, pl.ds(cls * HALF, HALF)], xbuf.at[mb, cls, 0], local_sem.at[4 + mb * 2 + cls]
            )
            for cls in range(2)
        ]
        for mb in range(micro)
    ]

    def w_copy(key):
        rows = rows_of(device_at(-key[0], key[1]), 0, width)
        return pltpu.make_async_copy(w_hbm.at[0, :, rows, :], w.at[:, rows, :], w_sem.at[slot(key)])

    barrier = pltpu.get_barrier_semaphore()
    for hop in (RIGHT, LEFT, ACROSS):
        pl.semaphore_signal(barrier, inc=1, device_id={"tp": device_at(*hop)}, device_id_type=MESH)
    pl.semaphore_signal(barrier, inc=1, device_id={"section": below}, device_id_type=MESH)
    pl.semaphore_signal(barrier, inc=1, device_id={"section": above}, device_id_type=MESH)
    for mb in range(micro):
        for cls in range(2):
            own_x[mb][cls].start()
    small[0].start()
    arrival = [(0, 0), (0, 1), (1, 0), (3, 0), (3, 1), (1, 1), (2, 0), (2, 1)]
    for key in arrival:
        w_copy(key).start()
    for copy in small[1:]:
        copy.start()

    place_r = lax.broadcasted_iota(jnp.int32, (128, 128), 0)
    place_c = lax.broadcasted_iota(jnp.int32, (128, 128), 1)
    small[0].wait()
    flip = jnp.where(lax.rem(place_r + place_c, 128) == 0, 1.0, 0.0).astype(F32)
    flipped[...] = jnp.dot(medium[...], flip, precision=lax.Precision.HIGHEST, preferred_element_type=F32)
    for part in range(3 * blocks):
        for mb in range(micro):
            proj[mb, part, 0:PAD, :] = jnp.zeros((PAD, 128), F32)
        turn[part, length : length + PAD, :] = jnp.zeros((PAD, 128), F32)
    for mb in range(micro):
        for cls in range(2):
            own_x[mb][cls].wait()

    pl.semaphore_wait(barrier, 5)

    sent = []

    def gather_copy(mb, cls, source, hop, key):
        return pltpu.make_async_remote_copy(
            src_ref=xbuf.at[mb, cls, slot(source)],
            dst_ref=xbuf.at[mb, cls, slot(key)],
            send_sem=ag_send.at[mb, cls, slot(key)],
            recv_sem=ag_recv.at[mb, cls, slot(key)],
            device_id={"tp": device_at(*hop)},
            device_id_type=MESH,
        )

    def origin(mb, cls, number):
        hop, key = ORIGIN[cls][number]
        copy = gather_copy(mb, cls, (0, 0), hop, key)
        copy.start()
        sent.append(copy)

    def handle(mb, cls, dx, dy):
        gather_copy(mb, cls, (0, 0), RIGHT, (dx, dy)).wait_recv()
        for hop, there in forwards(mb, cls, (dx, dy)):
            copy = gather_copy(mb, cls, (dx, dy), hop, there)
            copy.start()
            sent.append(copy)

    loaded, begun = set(), set()

    def project(mb, dx, dy):
        if (dx, dy) not in loaded:
            w_copy((dx, dy)).wait()
            loaded.add((dx, dy))
        rows = rows_of(device_at(-dx, dy), 0, width)
        chunk = jnp.concatenate([xbuf[mb, 0, slot((dx, dy))], xbuf[mb, 1, slot((dx, dy))]], axis=1)
        for stream in range(3):
            total = jnp.dot(chunk, w[stream, rows, :], preferred_element_type=F32)
            for block in range(blocks):
                piece = total[:, block * 128 : block * 128 + 128]
                where = (mb, stream * blocks + block, pl.ds(PAD, length), slice(None))
                proj[where] = proj[where] + piece if mb in begun else piece
        begun.add(mb)

    def build_tables(number):
        for group in range(4 * number, 4 * number + 4):
            rows = pl.ds(group * 128, 128)
            ahead = jnp.broadcast_to(medium[pl.ds(group, 1), :], (128, 128))
            ahead = pltpu.roll(ahead, 0, 1, stride=1, stride_axis=0)
            high, low = split_two(jnp.where(place_c >= place_r, ahead, 0.0))
            bwd_t[rows, 0:128] = high
            bwd_t[rows, 128:256] = low
            behind = jnp.broadcast_to(flipped[pl.ds(group, 1), :], (128, 128))
            behind = pltpu.roll(behind, 0, 1, stride=1, stride_axis=0)
            high, low = split_two(jnp.where(place_c <= place_r, behind, 0.0))
            fwd_t[rows, 0:128] = high
            fwd_t[rows, 128:256] = low

    def medium_conv(table, block, value):
        high, low = split_two(value)
        both = jnp.concatenate([high, low], axis=1)
        both = jnp.concatenate([both, both], axis=0)
        rows = pl.ds(block * 1024, 1024)
        raw = jnp.dot(table[rows, :], both, preferred_element_type=F32)
        lane_group = lax.div(place_c, 16)
        total = raw[0:length, 0:128] + raw[0:length, 128:256]
        for group in range(1, 8):
            first = group * 128
            piece = raw[first : first + length, 0:128] + raw[first : first + length, 128:256]
            total = jnp.where(lane_group == group, piece, total)
        return total

    ready = []

    def mixer(mb, half):
        while len(ready) < len(small) - 1:
            ready.append(small[len(ready) + 1].wait())

        def one_block(block):
            lanes = pl.ds(block * 128, 128)

            def featured(stream):
                total = jnp.zeros((length, 128), F32)
                for lag in range(7):
                    tap = taps[lag * 3 + stream, :, lanes]
                    total = total + tap * proj[mb, stream * blocks + block, pl.ds(PAD - lag, length), :]
                return total

            query, key, value = featured(0), featured(1), featured(2)
            gain = skip[:, lanes]
            product = key * value
            mixed = medium_conv(fwd_t, block, product) + gain * product
            upstream = inc[mb, :, lanes].astype(F32)
            mixed_grad = upstream * query
            product_grad = medium_conv(bwd_t, block, mixed_grad) + gain * mixed_grad
            turn[block, 0:length, :] = upstream * mixed
            turn[blocks + block, 0:length, :] = product_grad * value
            turn[2 * blocks + block, 0:length, :] = product_grad * key
            for stream in range(3):
                total = jnp.zeros((length, 128), F32)
                for lag in range(7):
                    tap = taps[lag * 3 + stream, :, lanes]
                    total = total + tap * turn[stream * blocks + block, pl.ds(lag, length), :]
                rows = pl.ds(stream * width + block * 128, 128)
                grad_t[mb, rows, :] = jnp.transpose(total).astype(BF16)

        for block in range(2 * half, 2 * half + 2):
            one_block(block)

    def sum_copy(mb, cls, key, hop):
        return pltpu.make_async_remote_copy(
            src_ref=sendbuf.at[mb, cls, slot(key)],
            dst_ref=recvbuf.at[mb, cls, slot(key)],
            send_sem=rs_send.at[mb, cls, slot(key)],
            recv_sem=rs_recv.at[mb, cls, slot(key)],
            device_id={"tp": device_at(*hop)},
            device_id_type=MESH,
        )

    def push_sum(mb, cls, key, hop, value):
        sendbuf[mb, cls, slot(key)] = value.astype(BF16)
        copy = sum_copy(mb, cls, key, hop)
        copy.start()
        sent.append(copy)

    def share(mb, dx, dy):
        key = (dx, dy)
        rows = rows_of(device_at(*key), 0, width)
        total = None
        for stream in range(3):
            part = jnp.dot(
                w[stream, rows, :], grad_t[mb, stream * width : stream * width + width, :], preferred_element_type=F32
            )
            total = part if total is None else total + part
        for cls in range(2):
            piece = total[cls * HALF : cls * HALF + HALF, :]
            hop, joins = returns(mb, cls, key)
            if hop is not None and not joins:
                push_sum(mb, cls, key, hop, piece)
            else:
                partial[mb, cls, slot(key)] = piece

    def combine(mb, cls, dx, dy):
        key = (dx, dy)
        hop, joins = returns(mb, cls, key)
        total = partial[mb, cls, slot(key)]
        for join in joins:
            sum_copy(mb, cls, join, RIGHT).wait_recv()
            total = total + recvbuf[mb, cls, slot(join)].astype(F32)
        if hop is not None:
            push_sum(mb, cls, key, hop, total)
            return
        upstream = inc[mb, :, cls * HALF : cls * HALF + HALF].astype(F32)
        final[mb, cls] = (jnp.transpose(total) + upstream).astype(BF16)
        copy = pltpu.make_async_remote_copy(
            src_ref=final.at[mb, cls],
            dst_ref=out_hbm.at[0, mb, :, pl.ds(cls * HALF, HALF)],
            send_sem=fin_send.at[mb, cls],
            recv_sem=fin_recv.at[mb, cls],
            device_id={"section": below},
            device_id_type=MESH,
        )
        copy.start()
        ended.append(copy)

    ended = []
    origin(1, 0, 1)
    origin(1, 1, 0)
    origin(0, 0, 1)
    origin(1, 1, 1)
    build_tables(7)
    origin(0, 1, 2)
    origin(0, 1, 0)
    build_tables(5)
    origin(1, 0, 0)
    origin(0, 0, 2)
    build_tables(4)
    origin(1, 0, 2)
    origin(0, 0, 0)
    origin(0, 1, 1)
    build_tables(2)
    handle(1, 0, 3, 0)
    handle(1, 1, 0, 1)
    handle(1, 1, 1, 0)
    handle(0, 1, 0, 1)
    project(1, 0, 0)
    origin(1, 1, 2)
    handle(0, 0, 3, 0)
    build_tables(3)
    project(0, 0, 0)
    handle(1, 0, 1, 0)
    build_tables(0)
    handle(1, 0, 2, 0)
    handle(1, 0, 0, 1)
    handle(0, 0, 0, 1)
    handle(0, 1, 1, 0)
    project(1, 0, 1)
    handle(0, 1, 3, 0)
    project(0, 0, 1)
    handle(1, 1, 3, 1)
    handle(1, 0, 3, 1)
    handle(0, 0, 1, 0)
    project(1, 3, 1)
    project(1, 1, 0)
    project(0, 1, 0)
    handle(0, 0, 3, 1)
    project(0, 3, 0)
    build_tables(6)
    handle(0, 1, 3, 1)
    project(0, 3, 1)
    build_tables(1)
    handle(1, 1, 1, 1)
    handle(1, 0, 1, 1)
    handle(1, 1, 2, 0)
    project(1, 1, 1)
    project(1, 2, 0)
    handle(1, 1, 3, 0)
    project(1, 3, 0)
    handle(1, 1, 2, 1)
    handle(1, 0, 2, 1)
    project(1, 2, 1)
    mixer(1, 0)
    mixer(1, 1)
    share(1, 2, 0)
    share(1, 2, 1)
    handle(0, 1, 2, 0)
    share(1, 1, 1)
    handle(0, 0, 1, 1)
    handle(0, 0, 2, 1)
    handle(0, 0, 2, 0)
    handle(0, 1, 1, 1)
    handle(0, 1, 2, 1)
    project(0, 1, 1)
    project(0, 2, 0)
    project(0, 2, 1)
    mixer(0, 0)
    mixer(0, 1)
    share(0, 2, 1)
    share(1, 3, 1)
    share(0, 2, 0)
    combine(1, 1, 3, 1)
    share(0, 3, 1)
    combine(1, 0, 2, 0)
    share(0, 1, 0)
    share(1, 0, 1)
    share(1, 1, 0)
    share(0, 1, 1)
    combine(0, 1, 3, 1)
    combine(0, 0, 1, 1)
    combine(1, 1, 1, 0)
    share(1, 3, 0)
    combine(1, 1, 0, 1)
    share(0, 0, 1)
    combine(1, 0, 1, 0)
    combine(1, 0, 3, 0)
    combine(0, 1, 1, 0)
    share(0, 3, 0)
    share(1, 0, 0)
    combine(0, 1, 0, 1)
    combine(0, 0, 3, 0)
    combine(0, 0, 1, 0)
    share(0, 0, 0)
    combine(1, 1, 0, 0)
    combine(1, 0, 0, 0)
    combine(0, 1, 0, 0)
    combine(0, 0, 0, 0)
    for copy in sent:
        copy.wait_send()
    for copy in ended:
        copy.wait()


def local(sections, block_input, incoming, in_weight, short_taps, medium_taps, skip_weight):
    _, micro, length, width = block_input.shape
    model_width = in_weight.shape[1]
    lags = short_taps.shape[1]
    groups = medium_taps.shape[2]
    weights = jnp.transpose(in_weight, (0, 2, 1, 3))
    taps = jnp.transpose(short_taps, (1, 2, 0, 3)).reshape(lags * 3, 1, width)
    medium = jnp.transpose(medium_taps, (0, 2, 1))
    parts = 3 * (width // 128)
    block_input, incoming, taps, medium, skip_weight = (
        pltpu.with_memory_space_constraint(value, pltpu.HBM)
        for value in (block_input, incoming, taps, medium, skip_weight)
    )
    anywhere = pl.BlockSpec(memory_space=pl.ANY)
    dma = pltpu.SemaphoreType.DMA
    return pl.pallas_call(
        functools.partial(kernel, sections),
        out_shape=jax.ShapeDtypeStruct(block_input.shape, BF16),
        in_specs=[anywhere] * 6,
        out_specs=anywhere,
        scratch_shapes=[
            pltpu.VMEM((micro, 2, 8, length, HALF), BF16),
            pltpu.VMEM((micro, length, width), BF16),
            pltpu.VMEM((3, model_width, width), BF16),
            pltpu.VMEM((lags * 3, 1, width), F32),
            pltpu.VMEM((groups, 128), F32),
            pltpu.VMEM((groups, 128), F32),
            pltpu.VMEM((1, width), F32),
            pltpu.VMEM((micro, parts, length + PAD, 128), F32),
            pltpu.VMEM((parts, length + PAD, 128), F32),
            pltpu.VMEM((micro, 3 * width, length), BF16),
            pltpu.VMEM((groups * 128, 256), BF16),
            pltpu.VMEM((groups * 128, 256), BF16),
            pltpu.VMEM((micro, 2, 8, HALF, length), F32),
            pltpu.VMEM((micro, 2, 8, HALF, length), BF16),
            pltpu.VMEM((micro, 2, 8, HALF, length), BF16),
            pltpu.VMEM((micro, 2, length, HALF), BF16),
            dma((8,)),
            dma((8,)),
            dma((micro, 2, 8)),
            dma((micro, 2, 8)),
            dma((micro, 2, 8)),
            dma((micro, 2, 8)),
            dma((micro, 2)),
            dma((micro, 2)),
        ],
        compiler_params=pltpu.CompilerParams(
            collective_id=0, has_side_effects=True, vmem_limit_bytes=48 * 1024 * 1024
        ),
    )(block_input, incoming, weights, taps, medium, skip_weight)


def solution(mesh):
    in_specs = (
        P("section", None, None, "tp"),
        P("section", None, None, "tp"),
        P("section", None, None, "tp"),
        P("section", None, None, "tp"),
        P("section", None, "tp"),
        P("section", "tp"),
    )
    out_specs = P("section", None, None, "tp")
    return jax.shard_map(
        functools.partial(local, mesh.shape["section"]),
        mesh=mesh, in_specs=in_specs, out_specs=out_specs, check_vma=False,
    )
```

```python
import functools

import jax
import jax.numpy as jnp
from jax import lax
from jax.experimental import pallas as pl
from jax.experimental.pallas import tpu as pltpu
from jax.sharding import PartitionSpec as P

MESH = pl.DeviceIdType.MESH
F32 = jnp.float32
BF16 = jnp.bfloat16
PAD = 8
HALF = 256
RIGHT, LEFT, ACROSS = (1, 0), (3, 0), (0, 1)

ORIGIN = {
    0: [(RIGHT, (1, 0)), (LEFT, (3, 0)), (ACROSS, (0, 1))],
    1: [(ACROSS, (0, 1)), (RIGHT, (1, 0)), (LEFT, (3, 0))],
}


def forwards(mb, cls, key):
    if cls == 0:
        far = RIGHT if mb == 0 else LEFT
        table = {
            (1, 0): [(ACROSS, (1, 1))],
            (3, 0): [(ACROSS, (3, 1))],
            (2, 0): [(ACROSS, (2, 1))],
        }
        table[far].insert(0, (far, (2, 0)))
        if mb == 0:
            del table[(2, 0)]
            table[(3, 1)] = [(LEFT, (2, 1))]
    else:
        table = {
            (0, 1): [(RIGHT, (1, 1)), (LEFT, (3, 1))],
            (1, 0): [(RIGHT, (2, 0))],
            (3, 1): [(LEFT, (2, 1))],
        }
    return table.get(key, [])


def returns(mb, cls, key):
    if cls == 0:
        far = RIGHT if mb == 0 else LEFT
        if mb == 0 and key == (2, 1):
            return RIGHT, []
        if key[1] == 1:
            return ACROSS, [(2, 1)] if mb == 0 and key == (1, 1) else []
        if key == (2, 0):
            return far, [] if mb == 0 else [(2, 1)]
        if key == (0, 0):
            return None, [(0, 1), (1, 0), (3, 0)]
        return key, [(key[0], 1)] + ([(2, 0)] if key == far else [])
    return {
        (2, 0): (RIGHT, []),
        (2, 1): (LEFT, []),
        (1, 1): (RIGHT, []),
        (3, 0): (LEFT, []),
        (1, 0): (RIGHT, [(2, 0)]),
        (3, 1): (LEFT, [(2, 1)]),
        (0, 1): (ACROSS, [(1, 1), (3, 1)]),
        (0, 0): (None, [(3, 0), (1, 0), (0, 1)]),
    }[key]


def slot(key):
    return key[0] * 2 + key[1]


def split_two(value):
    high = value.astype(BF16)
    low = (value - high.astype(F32)).astype(BF16)
    return high, low


def kernel(
    sections, x_hbm, inc_hbm, w_hbm, taps_hbm, medium_hbm, skip_hbm, out_hbm,
    xbuf, inc, w, taps, medium, flipped, skip, proj, turn, grad_t, fwd_t, bwd_t, partial, sendbuf, recvbuf, final,
    local_sem, w_sem, ag_send, ag_recv, rs_send, rs_recv, fin_send, fin_recv,
):
    me = lax.axis_index("tp")
    sec = lax.axis_index("section")
    below = lax.rem(sec + sections - 1, sections)
    above = lax.rem(sec + 1, sections)
    micro, length, width = inc.shape
    blocks = width // 128
    column, row = lax.div(me, 2), lax.rem(me, 2)

    def device_at(dx, dy):
        return lax.rem(column + 4 + dx, 4) * 2 + lax.rem(row + dy, 2)

    def rows_of(device, start, size):
        return pl.ds(pl.multiple_of(device * width + start, HALF), size)

    small = [
        pltpu.make_async_copy(medium_hbm.at[0], medium, local_sem.at[0]),
        pltpu.make_async_copy(taps_hbm, taps, local_sem.at[1]),
        pltpu.make_async_copy(skip_hbm, skip, local_sem.at[2]),
        pltpu.make_async_copy(inc_hbm.at[0], inc, local_sem.at[3]),
    ]
    own_x = [
        [
            pltpu.make_async_copy(
                x_hbm.at[0, mb, :, pl.ds(cls * HALF, HALF)], xbuf.at[mb, cls, 0], local_sem.at[4 + mb * 2 + cls]
            )
            for cls in range(2)
        ]
        for mb in range(micro)
    ]

    def w_copy(key):
        rows = rows_of(device_at(-key[0], key[1]), 0, width)
        return pltpu.make_async_copy(w_hbm.at[0, :, rows, :], w.at[:, rows, :], w_sem.at[slot(key)])

    barrier = pltpu.get_barrier_semaphore()
    for hop in (RIGHT, LEFT, ACROSS):
        pl.semaphore_signal(barrier, inc=1, device_id={"tp": device_at(*hop)}, device_id_type=MESH)
    pl.semaphore_signal(barrier, inc=1, device_id={"section": below}, device_id_type=MESH)
    pl.semaphore_signal(barrier, inc=1, device_id={"section": above}, device_id_type=MESH)
    for mb in range(micro):
        for cls in range(2):
            own_x[mb][cls].start()
    small[0].start()
    arrival = [(0, 0), (0, 1), (1, 0), (3, 0), (3, 1), (1, 1), (2, 0), (2, 1)]
    for key in arrival:
        w_copy(key).start()
    for copy in small[1:]:
        copy.start()

    place_r = lax.broadcasted_iota(jnp.int32, (128, 128), 0)
    place_c = lax.broadcasted_iota(jnp.int32, (128, 128), 1)
    for mb in range(micro):
        for cls in range(2):
            own_x[mb][cls].wait()

    pl.semaphore_wait(barrier, 5)

    sent = []

    def gather_copy(mb, cls, source, hop, key):
        return pltpu.make_async_remote_copy(
            src_ref=xbuf.at[mb, cls, slot(source)],
            dst_ref=xbuf.at[mb, cls, slot(key)],
            send_sem=ag_send.at[mb, cls, slot(key)],
            recv_sem=ag_recv.at[mb, cls, slot(key)],
            device_id={"tp": device_at(*hop)},
            device_id_type=MESH,
        )

    def origin(mb, cls, number):
        hop, key = ORIGIN[cls][number]
        copy = gather_copy(mb, cls, (0, 0), hop, key)
        copy.start()
        sent.append(copy)

    def handle(mb, cls, dx, dy):
        gather_copy(mb, cls, (0, 0), RIGHT, (dx, dy)).wait_recv()
        for hop, there in forwards(mb, cls, (dx, dy)):
            copy = gather_copy(mb, cls, (dx, dy), hop, there)
            copy.start()
            sent.append(copy)

    loaded, begun = set(), set()

    def project(mb, dx, dy):
        if (dx, dy) not in loaded:
            w_copy((dx, dy)).wait()
            loaded.add((dx, dy))
        rows = rows_of(device_at(-dx, dy), 0, width)
        chunk = jnp.concatenate([xbuf[mb, 0, slot((dx, dy))], xbuf[mb, 1, slot((dx, dy))]], axis=1)
        for stream in range(3):
            total = jnp.dot(chunk, w[stream, rows, :], preferred_element_type=F32)
            for block in range(blocks):
                piece = total[:, block * 128 : block * 128 + 128]
                where = (mb, stream * blocks + block, pl.ds(PAD, length), slice(None))
                proj[where] = proj[where] + piece if mb in begun else piece
        begun.add(mb)

    begun_tables = []

    def prepare():
        small[0].wait()
        flip = jnp.where(lax.rem(place_r + place_c, 128) == 0, 1.0, 0.0).astype(F32)
        flipped[...] = jnp.dot(medium[...], flip, precision=lax.Precision.HIGHEST, preferred_element_type=F32)
        for part in range(3 * blocks):
            for mb in range(micro):
                proj[mb, part, 0:PAD, :] = jnp.zeros((PAD, 128), F32)
            turn[part, length : length + PAD, :] = jnp.zeros((PAD, 128), F32)

    def build_tables(number):
        if not begun_tables:
            prepare()
            begun_tables.append(number)
        for group in range(4 * number, 4 * number + 4):
            rows = pl.ds(group * 128, 128)
            ahead = jnp.broadcast_to(medium[pl.ds(group, 1), :], (128, 128))
            ahead = pltpu.roll(ahead, 0, 1, stride=1, stride_axis=0)
            high, low = split_two(jnp.where(place_c >= place_r, ahead, 0.0))
            bwd_t[rows, 0:128] = high
            bwd_t[rows, 128:256] = low
            behind = jnp.broadcast_to(flipped[pl.ds(group, 1), :], (128, 128))
            behind = pltpu.roll(behind, 0, 1, stride=1, stride_axis=0)
            high, low = split_two(jnp.where(place_c <= place_r, behind, 0.0))
            fwd_t[rows, 0:128] = high
            fwd_t[rows, 128:256] = low

    def medium_conv(table, block, value):
        high, low = split_two(value)
        both = jnp.concatenate([high, low], axis=1)
        both = jnp.concatenate([both, both], axis=0)
        rows = pl.ds(block * 1024, 1024)
        raw = jnp.dot(table[rows, :], both, preferred_element_type=F32)
        lane_group = lax.div(place_c, 16)
        total = raw[0:length, 0:128] + raw[0:length, 128:256]
        for group in range(1, 8):
            first = group * 128
            piece = raw[first : first + length, 0:128] + raw[first : first + length, 128:256]
            total = jnp.where(lane_group == group, piece, total)
        return total

    ready = []

    def mixer(mb, half):
        while len(ready) < len(small) - 1:
            ready.append(small[len(ready) + 1].wait())

        def one_block(block):
            lanes = pl.ds(block * 128, 128)

            def featured(stream):
                total = jnp.zeros((length, 128), F32)
                for lag in range(7):
                    tap = taps[lag * 3 + stream, :, lanes]
                    total = total + tap * proj[mb, stream * blocks + block, pl.ds(PAD - lag, length), :]
                return total

            query, key, value = featured(0), featured(1), featured(2)
            gain = skip[:, lanes]
            product = key * value
            mixed = medium_conv(fwd_t, block, product) + gain * product
            upstream = inc[mb, :, lanes].astype(F32)
            mixed_grad = upstream * query
            product_grad = medium_conv(bwd_t, block, mixed_grad) + gain * mixed_grad
            turn[block, 0:length, :] = upstream * mixed
            turn[blocks + block, 0:length, :] = product_grad * value
            turn[2 * blocks + block, 0:length, :] = product_grad * key
            for stream in range(3):
                total = jnp.zeros((length, 128), F32)
                for lag in range(7):
                    tap = taps[lag * 3 + stream, :, lanes]
                    total = total + tap * turn[stream * blocks + block, pl.ds(lag, length), :]
                rows = pl.ds(stream * width + block * 128, 128)
                grad_t[mb, rows, :] = jnp.transpose(total).astype(BF16)

        for block in range(2 * half, 2 * half + 2):
            one_block(block)

    def sum_copy(mb, cls, key, hop):
        return pltpu.make_async_remote_copy(
            src_ref=sendbuf.at[mb, cls, slot(key)],
            dst_ref=recvbuf.at[mb, cls, slot(key)],
            send_sem=rs_send.at[mb, cls, slot(key)],
            recv_sem=rs_recv.at[mb, cls, slot(key)],
            device_id={"tp": device_at(*hop)},
            device_id_type=MESH,
        )

    def push_sum(mb, cls, key, hop, value):
        sendbuf[mb, cls, slot(key)] = value.astype(BF16)
        copy = sum_copy(mb, cls, key, hop)
        copy.start()
        sent.append(copy)

    def share(mb, dx, dy):
        key = (dx, dy)
        rows = rows_of(device_at(*key), 0, width)
        total = None
        for stream in range(3):
            part = jnp.dot(
                w[stream, rows, :], grad_t[mb, stream * width : stream * width + width, :], preferred_element_type=F32
            )
            total = part if total is None else total + part
        for cls in range(2):
            piece = total[cls * HALF : cls * HALF + HALF, :]
            hop, joins = returns(mb, cls, key)
            if hop is not None and not joins:
                push_sum(mb, cls, key, hop, piece)
            else:
                partial[mb, cls, slot(key)] = piece

    def combine(mb, cls, dx, dy):
        key = (dx, dy)
        hop, joins = returns(mb, cls, key)
        total = partial[mb, cls, slot(key)]
        for join in joins:
            sum_copy(mb, cls, join, RIGHT).wait_recv()
            total = total + recvbuf[mb, cls, slot(join)].astype(F32)
        if hop is not None:
            push_sum(mb, cls, key, hop, total)
            return
        upstream = inc[mb, :, cls * HALF : cls * HALF + HALF].astype(F32)
        final[mb, cls] = (jnp.transpose(total) + upstream).astype(BF16)
        copy = pltpu.make_async_remote_copy(
            src_ref=final.at[mb, cls],
            dst_ref=out_hbm.at[0, mb, :, pl.ds(cls * HALF, HALF)],
            send_sem=fin_send.at[mb, cls],
            recv_sem=fin_recv.at[mb, cls],
            device_id={"section": below},
            device_id_type=MESH,
        )
        copy.start()
        ended.append(copy)

    ended = []
    origin(1, 0, 1)
    origin(1, 1, 0)
    origin(0, 0, 1)
    origin(1, 1, 1)
    build_tables(7)
    origin(0, 1, 2)
    origin(0, 1, 0)
    build_tables(5)
    origin(1, 0, 0)
    origin(0, 0, 2)
    build_tables(4)
    origin(1, 0, 2)
    origin(0, 0, 0)
    origin(0, 1, 1)
    build_tables(2)
    handle(1, 0, 3, 0)
    handle(1, 1, 0, 1)
    handle(1, 1, 1, 0)
    handle(0, 1, 0, 1)
    project(1, 0, 0)
    origin(1, 1, 2)
    handle(0, 0, 3, 0)
    build_tables(3)
    project(0, 0, 0)
    handle(1, 0, 1, 0)
    build_tables(0)
    handle(1, 0, 2, 0)
    handle(1, 0, 0, 1)
    handle(0, 0, 0, 1)
    handle(0, 1, 1, 0)
    project(1, 0, 1)
    handle(0, 1, 3, 0)
    project(0, 0, 1)
    handle(1, 1, 3, 1)
    handle(1, 0, 3, 1)
    handle(0, 0, 1, 0)
    project(1, 3, 1)
    project(1, 1, 0)
    project(0, 1, 0)
    handle(0, 0, 3, 1)
    project(0, 3, 0)
    build_tables(6)
    handle(0, 1, 3, 1)
    project(0, 3, 1)
    build_tables(1)
    handle(1, 1, 1, 1)
    handle(1, 0, 1, 1)
    handle(1, 1, 2, 0)
    project(1, 1, 1)
    project(1, 2, 0)
    handle(1, 1, 3, 0)
    project(1, 3, 0)
    handle(1, 1, 2, 1)
    handle(1, 0, 2, 1)
    project(1, 2, 1)
    mixer(1, 0)
    mixer(1, 1)
    share(1, 2, 0)
    share(1, 2, 1)
    handle(0, 1, 2, 0)
    share(1, 1, 1)
    handle(0, 0, 1, 1)
    handle(0, 0, 2, 1)
    handle(0, 0, 2, 0)
    handle(0, 1, 1, 1)
    handle(0, 1, 2, 1)
    project(0, 1, 1)
    project(0, 2, 0)
    project(0, 2, 1)
    mixer(0, 0)
    mixer(0, 1)
    share(0, 2, 1)
    share(1, 3, 1)
    share(0, 2, 0)
    combine(1, 1, 3, 1)
    share(0, 3, 1)
    combine(1, 0, 2, 0)
    share(0, 1, 0)
    share(1, 0, 1)
    share(1, 1, 0)
    share(0, 1, 1)
    combine(0, 1, 3, 1)
    combine(0, 0, 1, 1)
    combine(1, 1, 1, 0)
    share(1, 3, 0)
    combine(1, 1, 0, 1)
    share(0, 0, 1)
    combine(1, 0, 1, 0)
    combine(1, 0, 3, 0)
    combine(0, 1, 1, 0)
    share(0, 3, 0)
    share(1, 0, 0)
    combine(0, 1, 0, 1)
    combine(0, 0, 3, 0)
    combine(0, 0, 1, 0)
    share(0, 0, 0)
    combine(1, 1, 0, 0)
    combine(1, 0, 0, 0)
    combine(0, 1, 0, 0)
    combine(0, 0, 0, 0)
    for copy in sent:
        copy.wait_send()
    for copy in ended:
        copy.wait()


def local(sections, block_input, incoming, in_weight, short_taps, medium_taps, skip_weight):
    _, micro, length, width = block_input.shape
    model_width = in_weight.shape[1]
    lags = short_taps.shape[1]
    groups = medium_taps.shape[2]
    weights = jnp.transpose(in_weight, (0, 2, 1, 3))
    taps = jnp.transpose(short_taps, (1, 2, 0, 3)).reshape(lags * 3, 1, width)
    medium = jnp.transpose(medium_taps, (0, 2, 1))
    parts = 3 * (width // 128)
    block_input, incoming, taps, medium, skip_weight = (
        pltpu.with_memory_space_constraint(value, pltpu.HBM)
        for value in (block_input, incoming, taps, medium, skip_weight)
    )
    anywhere = pl.BlockSpec(memory_space=pl.ANY)
    dma = pltpu.SemaphoreType.DMA
    return pl.pallas_call(
        functools.partial(kernel, sections),
        out_shape=jax.ShapeDtypeStruct(block_input.shape, BF16),
        in_specs=[anywhere] * 6,
        out_specs=anywhere,
        scratch_shapes=[
            pltpu.VMEM((micro, 2, 8, length, HALF), BF16),
            pltpu.VMEM((micro, length, width), BF16),
            pltpu.VMEM((3, model_width, width), BF16),
            pltpu.VMEM((lags * 3, 1, width), F32),
            pltpu.VMEM((groups, 128), F32),
            pltpu.VMEM((groups, 128), F32),
            pltpu.VMEM((1, width), F32),
            pltpu.VMEM((micro, parts, length + PAD, 128), F32),
            pltpu.VMEM((parts, length + PAD, 128), F32),
            pltpu.VMEM((micro, 3 * width, length), BF16),
            pltpu.VMEM((groups * 128, 256), BF16),
            pltpu.VMEM((groups * 128, 256), BF16),
            pltpu.VMEM((micro, 2, 8, HALF, length), F32),
            pltpu.VMEM((micro, 2, 8, HALF, length), BF16),
            pltpu.VMEM((micro, 2, 8, HALF, length), BF16),
            pltpu.VMEM((micro, 2, length, HALF), BF16),
            dma((8,)),
            dma((8,)),
            dma((micro, 2, 8)),
            dma((micro, 2, 8)),
            dma((micro, 2, 8)),
            dma((micro, 2, 8)),
            dma((micro, 2)),
            dma((micro, 2)),
        ],
        compiler_params=pltpu.CompilerParams(
            collective_id=0, has_side_effects=True, vmem_limit_bytes=48 * 1024 * 1024
        ),
    )(block_input, incoming, weights, taps, medium, skip_weight)


def solution(mesh):
    in_specs = (
        P("section", None, None, "tp"),
        P("section", None, None, "tp"),
        P("section", None, None, "tp"),
        P("section", None, None, "tp"),
        P("section", None, "tp"),
        P("section", "tp"),
    )
    out_specs = P("section", None, None, "tp")
    return jax.shard_map(
        functools.partial(local, mesh.shape["section"]),
        mesh=mesh, in_specs=in_specs, out_specs=out_specs, check_vma=False,
    )
```

```python
import functools

import jax
import jax.numpy as jnp
from jax import lax
from jax.experimental import pallas as pl
from jax.experimental.pallas import tpu as pltpu
from jax.sharding import PartitionSpec as P

MESH = pl.DeviceIdType.MESH
F32 = jnp.float32
BF16 = jnp.bfloat16
PAD = 8
HALF = 256
RIGHT, LEFT, ACROSS = (1, 0), (3, 0), (0, 1)

ORIGIN = {
    0: [(RIGHT, (1, 0)), (LEFT, (3, 0)), (ACROSS, (0, 1))],
    1: [(ACROSS, (0, 1)), (RIGHT, (1, 0)), (LEFT, (3, 0))],
}


def forwards(mb, cls, key):
    if cls == 0:
        far = RIGHT if mb == 0 else LEFT
        table = {
            (1, 0): [(ACROSS, (1, 1))],
            (3, 0): [(ACROSS, (3, 1))],
            (2, 0): [(ACROSS, (2, 1))],
        }
        table[far].insert(0, (far, (2, 0)))
        if mb == 0:
            del table[(2, 0)]
            table[(3, 1)] = [(LEFT, (2, 1))]
    else:
        table = {
            (0, 1): [(RIGHT, (1, 1)), (LEFT, (3, 1))],
            (1, 0): [(RIGHT, (2, 0))],
            (3, 1): [(LEFT, (2, 1))],
        }
    return table.get(key, [])


def returns(mb, cls, key):
    if cls == 0:
        far = RIGHT if mb == 0 else LEFT
        if mb == 0 and key == (2, 1):
            return RIGHT, []
        if key[1] == 1:
            return ACROSS, [(2, 1)] if mb == 0 and key == (1, 1) else []
        if key == (2, 0):
            return far, [] if mb == 0 else [(2, 1)]
        if key == (0, 0):
            return None, [(0, 1), (1, 0), (3, 0)]
        return key, [(key[0], 1)] + ([(2, 0)] if key == far else [])
    return {
        (2, 0): (RIGHT, []),
        (2, 1): (LEFT, []),
        (1, 1): (RIGHT, []),
        (3, 0): (LEFT, []),
        (1, 0): (RIGHT, [(2, 0)]),
        (3, 1): (LEFT, [(2, 1)]),
        (0, 1): (ACROSS, [(1, 1), (3, 1)]),
        (0, 0): (None, [(3, 0), (1, 0), (0, 1)]),
    }[key]


def slot(key):
    return key[0] * 2 + key[1]


def split_two(value):
    high = value.astype(BF16)
    low = (value - high.astype(F32)).astype(BF16)
    return high, low


def kernel(
    sections, x_hbm, inc_hbm, w_hbm, taps_hbm, medium_hbm, skip_hbm, out_hbm,
    xbuf, inc, w, taps, medium, flipped, skip, proj, turn, grad_t, fwd_t, bwd_t, partial, sendbuf, recvbuf, final,
    local_sem, w_sem, ag_send, ag_recv, rs_send, rs_recv, fin_send, fin_recv,
):
    me = lax.axis_index("tp")
    sec = lax.axis_index("section")
    below = lax.rem(sec + sections - 1, sections)
    above = lax.rem(sec + 1, sections)
    micro, length, width = inc.shape
    blocks = width // 128
    column, row = lax.div(me, 2), lax.rem(me, 2)

    def device_at(dx, dy):
        return lax.rem(column + 4 + dx, 4) * 2 + lax.rem(row + dy, 2)

    def rows_of(device, start, size):
        return pl.ds(pl.multiple_of(device * width + start, HALF), size)

    small = [
        pltpu.make_async_copy(medium_hbm.at[0], medium, local_sem.at[0]),
        pltpu.make_async_copy(taps_hbm, taps, local_sem.at[1]),
        pltpu.make_async_copy(skip_hbm, skip, local_sem.at[2]),
        pltpu.make_async_copy(inc_hbm.at[0], inc, local_sem.at[3]),
    ]
    own_x = [
        [
            pltpu.make_async_copy(
                x_hbm.at[0, mb, :, pl.ds(cls * HALF, HALF)], xbuf.at[mb, cls, 0], local_sem.at[4 + mb * 2 + cls]
            )
            for cls in range(2)
        ]
        for mb in range(micro)
    ]

    def w_copy(key):
        rows = rows_of(device_at(-key[0], key[1]), 0, width)
        return pltpu.make_async_copy(w_hbm.at[0, :, rows, :], w.at[:, rows, :], w_sem.at[slot(key)])

    barrier = pltpu.get_barrier_semaphore()
    for hop in (RIGHT, LEFT, ACROSS):
        pl.semaphore_signal(barrier, inc=1, device_id={"tp": device_at(*hop)}, device_id_type=MESH)
    pl.semaphore_signal(barrier, inc=1, device_id={"section": below}, device_id_type=MESH)
    pl.semaphore_signal(barrier, inc=1, device_id={"section": above}, device_id_type=MESH)
    for mb in range(micro):
        for cls in range(2):
            own_x[mb][cls].start()
    small[0].start()
    arrival = [(0, 0), (0, 1), (1, 0), (3, 0), (3, 1), (1, 1), (2, 0), (2, 1)]
    for key in arrival:
        w_copy(key).start()
    for copy in small[1:]:
        copy.start()

    place_r = lax.broadcasted_iota(jnp.int32, (128, 128), 0)
    place_c = lax.broadcasted_iota(jnp.int32, (128, 128), 1)
    for mb in range(micro):
        for cls in range(2):
            own_x[mb][cls].wait()

    pl.semaphore_wait(barrier, 5)

    sent = []

    def gather_copy(mb, cls, source, hop, key):
        return pltpu.make_async_remote_copy(
            src_ref=xbuf.at[mb, cls, slot(source)],
            dst_ref=xbuf.at[mb, cls, slot(key)],
            send_sem=ag_send.at[mb, cls, slot(key)],
            recv_sem=ag_recv.at[mb, cls, slot(key)],
            device_id={"tp": device_at(*hop)},
            device_id_type=MESH,
        )

    def origin(mb, cls, number):
        hop, key = ORIGIN[cls][number]
        copy = gather_copy(mb, cls, (0, 0), hop, key)
        copy.start()
        sent.append(copy)

    def handle(mb, cls, dx, dy):
        gather_copy(mb, cls, (0, 0), RIGHT, (dx, dy)).wait_recv()
        for hop, there in forwards(mb, cls, (dx, dy)):
            copy = gather_copy(mb, cls, (dx, dy), hop, there)
            copy.start()
            sent.append(copy)

    loaded, begun = set(), set()

    def project(mb, dx, dy):
        if (dx, dy) not in loaded:
            w_copy((dx, dy)).wait()
            loaded.add((dx, dy))
        rows = rows_of(device_at(-dx, dy), 0, width)
        chunk = jnp.concatenate([xbuf[mb, 0, slot((dx, dy))], xbuf[mb, 1, slot((dx, dy))]], axis=1)
        for stream in range(3):
            total = jnp.dot(chunk, w[stream, rows, :], preferred_element_type=F32)
            for block in range(blocks):
                piece = total[:, block * 128 : block * 128 + 128]
                where = (mb, stream * blocks + block, pl.ds(PAD, length), slice(None))
                proj[where] = proj[where] + piece if mb in begun else piece
        begun.add(mb)

    begun_tables = []

    def prepare():
        small[0].wait()
        flip = jnp.where(lax.rem(place_r + place_c, 128) == 0, 1.0, 0.0).astype(F32)
        flipped[...] = jnp.dot(medium[...], flip, precision=lax.Precision.HIGHEST, preferred_element_type=F32)
        for part in range(3 * blocks):
            for mb in range(micro):
                proj[mb, part, 0:PAD, :] = jnp.zeros((PAD, 128), F32)
            turn[part, length : length + PAD, :] = jnp.zeros((PAD, 128), F32)

    def build_tables(number):
        if not begun_tables:
            prepare()
            begun_tables.append(number)
        for group in range(4 * number, 4 * number + 4):
            rows = pl.ds(group * 128, 128)
            ahead = jnp.broadcast_to(medium[pl.ds(group, 1), :], (128, 128))
            ahead = pltpu.roll(ahead, 0, 1, stride=1, stride_axis=0)
            high, low = split_two(jnp.where(place_c >= place_r, ahead, 0.0))
            bwd_t[rows, 0:128] = high
            bwd_t[rows, 128:256] = low
            behind = jnp.broadcast_to(flipped[pl.ds(group, 1), :], (128, 128))
            behind = pltpu.roll(behind, 0, 1, stride=1, stride_axis=0)
            high, low = split_two(jnp.where(place_c <= place_r, behind, 0.0))
            fwd_t[rows, 0:128] = high
            fwd_t[rows, 128:256] = low

    def medium_conv(table, block, value):
        high, low = split_two(value)
        both = jnp.concatenate([high, low], axis=1)
        both = jnp.concatenate([both, both], axis=0)
        rows = pl.ds(block * 1024, 1024)
        raw = jnp.dot(table[rows, :], both, preferred_element_type=F32)
        lane_group = lax.div(place_c, 16)
        total = raw[0:length, 0:128] + raw[0:length, 128:256]
        for group in range(1, 8):
            first = group * 128
            piece = raw[first : first + length, 0:128] + raw[first : first + length, 128:256]
            total = jnp.where(lane_group == group, piece, total)
        return total

    ready = []

    def mixer(mb, half):
        while len(ready) < len(small) - 1:
            ready.append(small[len(ready) + 1].wait())

        def one_block(block):
            lanes = pl.ds(block * 128, 128)

            def featured(stream):
                total = jnp.zeros((length, 128), F32)
                for lag in range(7):
                    tap = taps[lag * 3 + stream, :, lanes]
                    total = total + tap * proj[mb, stream * blocks + block, pl.ds(PAD - lag, length), :]
                return total

            query, key, value = featured(0), featured(1), featured(2)
            gain = skip[:, lanes]
            product = key * value
            mixed = medium_conv(fwd_t, block, product) + gain * product
            upstream = inc[mb, :, lanes].astype(F32)
            mixed_grad = upstream * query
            product_grad = medium_conv(bwd_t, block, mixed_grad) + gain * mixed_grad
            turn[block, 0:length, :] = upstream * mixed
            turn[blocks + block, 0:length, :] = product_grad * value
            turn[2 * blocks + block, 0:length, :] = product_grad * key
            for stream in range(3):
                total = jnp.zeros((length, 128), F32)
                for lag in range(7):
                    tap = taps[lag * 3 + stream, :, lanes]
                    total = total + tap * turn[stream * blocks + block, pl.ds(lag, length), :]
                rows = pl.ds(stream * width + block * 128, 128)
                grad_t[mb, rows, :] = jnp.transpose(total).astype(BF16)

        for block in range(2 * half, 2 * half + 2):
            one_block(block)

    def sum_copy(mb, cls, key, hop):
        return pltpu.make_async_remote_copy(
            src_ref=sendbuf.at[mb, cls, slot(key)],
            dst_ref=recvbuf.at[mb, cls, slot(key)],
            send_sem=rs_send.at[mb, cls, slot(key)],
            recv_sem=rs_recv.at[mb, cls, slot(key)],
            device_id={"tp": device_at(*hop)},
            device_id_type=MESH,
        )

    def push_sum(mb, cls, key, hop, value):
        sendbuf[mb, cls, slot(key)] = value.astype(BF16)
        copy = sum_copy(mb, cls, key, hop)
        copy.start()
        sent.append(copy)

    def share(mb, dx, dy):
        key = (dx, dy)
        rows = rows_of(device_at(*key), 0, width)
        total = None
        for stream in range(3):
            part = jnp.dot(
                w[stream, rows, :], grad_t[mb, stream * width : stream * width + width, :], preferred_element_type=F32
            )
            total = part if total is None else total + part
        for cls in range(2):
            piece = total[cls * HALF : cls * HALF + HALF, :]
            hop, joins = returns(mb, cls, key)
            if hop is not None and not joins:
                push_sum(mb, cls, key, hop, piece)
            else:
                partial[mb, cls, slot(key)] = piece

    def combine(mb, cls, dx, dy):
        key = (dx, dy)
        hop, joins = returns(mb, cls, key)
        total = partial[mb, cls, slot(key)]
        for join in joins:
            sum_copy(mb, cls, join, RIGHT).wait_recv()
            total = total + recvbuf[mb, cls, slot(join)].astype(F32)
        if hop is not None:
            push_sum(mb, cls, key, hop, total)
            return
        upstream = inc[mb, :, cls * HALF : cls * HALF + HALF].astype(F32)
        final[mb, cls] = (jnp.transpose(total) + upstream).astype(BF16)
        copy = pltpu.make_async_remote_copy(
            src_ref=final.at[mb, cls],
            dst_ref=out_hbm.at[0, mb, :, pl.ds(cls * HALF, HALF)],
            send_sem=fin_send.at[mb, cls],
            recv_sem=fin_recv.at[mb, cls],
            device_id={"section": below},
            device_id_type=MESH,
        )
        copy.start()
        ended.append(copy)

    ended = []
    origin(1, 0, 1)
    origin(1, 1, 0)
    origin(0, 0, 1)
    origin(1, 1, 1)
    origin(0, 1, 2)
    origin(0, 1, 0)
    build_tables(5)
    origin(1, 0, 0)
    build_tables(7)
    origin(0, 0, 2)
    build_tables(4)
    origin(1, 0, 2)
    origin(0, 0, 0)
    origin(0, 1, 1)
    build_tables(2)
    handle(1, 0, 3, 0)
    handle(1, 1, 0, 1)
    handle(1, 1, 1, 0)
    handle(0, 1, 0, 1)
    project(1, 0, 0)
    origin(1, 1, 2)
    handle(0, 0, 3, 0)
    build_tables(3)
    project(0, 0, 0)
    handle(1, 0, 1, 0)
    build_tables(0)
    handle(1, 0, 2, 0)
    handle(1, 0, 0, 1)
    handle(0, 0, 0, 1)
    handle(0, 1, 1, 0)
    project(1, 0, 1)
    handle(0, 1, 3, 0)
    project(0, 0, 1)
    handle(1, 1, 3, 1)
    handle(1, 0, 3, 1)
    handle(0, 0, 1, 0)
    project(1, 3, 1)
    project(1, 1, 0)
    project(0, 1, 0)
    handle(0, 0, 3, 1)
    project(0, 3, 0)
    build_tables(6)
    handle(0, 1, 3, 1)
    project(0, 3, 1)
    build_tables(1)
    handle(1, 1, 1, 1)
    handle(1, 0, 1, 1)
    handle(1, 1, 2, 0)
    project(1, 1, 1)
    project(1, 2, 0)
    handle(1, 1, 3, 0)
    project(1, 3, 0)
    handle(1, 1, 2, 1)
    handle(1, 0, 2, 1)
    project(1, 2, 1)
    mixer(1, 0)
    mixer(1, 1)
    share(1, 2, 0)
    share(1, 2, 1)
    handle(0, 1, 2, 0)
    share(1, 1, 1)
    handle(0, 0, 1, 1)
    handle(0, 0, 2, 1)
    handle(0, 0, 2, 0)
    handle(0, 1, 1, 1)
    handle(0, 1, 2, 1)
    project(0, 1, 1)
    project(0, 2, 0)
    project(0, 2, 1)
    mixer(0, 0)
    mixer(0, 1)
    share(0, 2, 1)
    share(1, 3, 1)
    share(0, 2, 0)
    combine(1, 1, 3, 1)
    share(0, 3, 1)
    combine(1, 0, 2, 0)
    share(0, 1, 0)
    share(1, 0, 1)
    share(1, 1, 0)
    share(0, 1, 1)
    combine(0, 1, 3, 1)
    combine(0, 0, 1, 1)
    combine(1, 1, 1, 0)
    share(1, 3, 0)
    combine(1, 1, 0, 1)
    share(0, 0, 1)
    combine(1, 0, 1, 0)
    combine(1, 0, 3, 0)
    combine(0, 1, 1, 0)
    share(0, 3, 0)
    share(1, 0, 0)
    combine(0, 1, 0, 1)
    combine(0, 0, 3, 0)
    combine(0, 0, 1, 0)
    share(0, 0, 0)
    combine(1, 1, 0, 0)
    combine(1, 0, 0, 0)
    combine(0, 1, 0, 0)
    combine(0, 0, 0, 0)
    for copy in sent:
        copy.wait_send()
    for copy in ended:
        copy.wait()


def local(sections, block_input, incoming, in_weight, short_taps, medium_taps, skip_weight):
    _, micro, length, width = block_input.shape
    model_width = in_weight.shape[1]
    lags = short_taps.shape[1]
    groups = medium_taps.shape[2]
    weights = jnp.transpose(in_weight, (0, 2, 1, 3))
    taps = jnp.transpose(short_taps, (1, 2, 0, 3)).reshape(lags * 3, 1, width)
    medium = jnp.transpose(medium_taps, (0, 2, 1))
    parts = 3 * (width // 128)
    block_input, incoming, taps, medium, skip_weight = (
        pltpu.with_memory_space_constraint(value, pltpu.HBM)
        for value in (block_input, incoming, taps, medium, skip_weight)
    )
    anywhere = pl.BlockSpec(memory_space=pl.ANY)
    dma = pltpu.SemaphoreType.DMA
    return pl.pallas_call(
        functools.partial(kernel, sections),
        out_shape=jax.ShapeDtypeStruct(block_input.shape, BF16),
        in_specs=[anywhere] * 6,
        out_specs=anywhere,
        scratch_shapes=[
            pltpu.VMEM((micro, 2, 8, length, HALF), BF16),
            pltpu.VMEM((micro, length, width), BF16),
            pltpu.VMEM((3, model_width, width), BF16),
            pltpu.VMEM((lags * 3, 1, width), F32),
            pltpu.VMEM((groups, 128), F32),
            pltpu.VMEM((groups, 128), F32),
            pltpu.VMEM((1, width), F32),
            pltpu.VMEM((micro, parts, length + PAD, 128), F32),
            pltpu.VMEM((parts, length + PAD, 128), F32),
            pltpu.VMEM((micro, 3 * width, length), BF16),
            pltpu.VMEM((groups * 128, 256), BF16),
            pltpu.VMEM((groups * 128, 256), BF16),
            pltpu.VMEM((micro, 2, 8, HALF, length), F32),
            pltpu.VMEM((micro, 2, 8, HALF, length), BF16),
            pltpu.VMEM((micro, 2, 8, HALF, length), BF16),
            pltpu.VMEM((micro, 2, length, HALF), BF16),
            dma((8,)),
            dma((8,)),
            dma((micro, 2, 8)),
            dma((micro, 2, 8)),
            dma((micro, 2, 8)),
            dma((micro, 2, 8)),
            dma((micro, 2)),
            dma((micro, 2)),
        ],
        compiler_params=pltpu.CompilerParams(
            collective_id=0, has_side_effects=True, vmem_limit_bytes=48 * 1024 * 1024
        ),
    )(block_input, incoming, weights, taps, medium, skip_weight)


def solution(mesh):
    in_specs = (
        P("section", None, None, "tp"),
        P("section", None, None, "tp"),
        P("section", None, None, "tp"),
        P("section", None, None, "tp"),
        P("section", None, "tp"),
        P("section", "tp"),
    )
    out_specs = P("section", None, None, "tp")
    return jax.shard_map(
        functools.partial(local, mesh.shape["section"]),
        mesh=mesh, in_specs=in_specs, out_specs=out_specs, check_vma=False,
    )
```
